512 devices in a mesh: dp: 32 (over x, z_hi, core), space: 16 (over y, z_lo).
Axes of the slice: x: 4, y: 4, z: 16 (z_hi: 4, z_lo: 4; z = z_hi * 4 + z_lo), core: 2. Of those that a mesh axis runs over, the one named last changes fastest.
Arguments:
- field: bfloat16 [32, 64, 32, 16, 128], P('dp', 'space'), may hold values from -6 to 6
- cotangent: bfloat16 [32, 64, 32, 16, 128], P('dp', 'space'), may hold values from -6 to 6
- weights: float32 [16, 128, 2, 128, 128], P('space', 'dp'), may hold values from -0.375 to 0.375
- first_moment: float32 [16, 128, 2, 128, 128], P('space', 'dp'), may hold values from -6 to 6
- second_moment: float32 [16, 128, 2, 128, 128], P('space', 'dp'), may hold values from 0.01 to 10
Outputs:
- field_grad: bfloat16 [32, 64, 32, 16, 128], P('dp', 'space')
- new_weights: float32 [16, 128, 2, 128, 128], P('space', 'dp')
- new_first: float32 [16, 128, 2, 128, 128], P('space', 'dp')
- new_second: float32 [16, 128, 2, 128, 128], P('space', 'dp')
The draws below stay inside these ranges and needn't reach their ends.
All inputs are finite; a program needn't handle non-finite values.
Results may differ from the reference program's by a relative error of at most 0.024.
Values may be sent and summed in bfloat16 or wider, within the bound.
A program may use at most 64 MiB of HBM per device.

```python
import math
import jax
import jax.numpy as jnp
from jax import lax

C = 128
MX = 16
MY = 16
MZ = 8
NY = 32
NZ = 16
STEP = 100
MYZ = 128
NX = 64
BATCH = 32


def block_levels(rng, dims, split, low, high):
    level, own = 1.0, jax.random.fold_in(rng, 6)
    for dim, parts in split:
        draws = jnp.exp(jax.random.uniform(jax.random.fold_in(own, dim), (parts,), jnp.float32, low / len(split), high / len(split)))
        level = level * jnp.repeat(draws, dims[dim] // parts).reshape([-1 if axis == dim else 1 for axis in range(len(dims))])
    return level


def normal_values(own_key, dims, deviation, bound, split=(), kind=jnp.bfloat16):
    gain = block_levels(own_key, dims, split, -0.22, 0.18) if split else 1.0
    entries = jax.random.normal(own_key, dims, jnp.float32) * deviation * gain
    return jnp.minimum(jnp.maximum(entries, -bound), bound).astype(kind)


def setup_inputs(seed: int = 0) -> dict:
    key_list = jax.random.split(jax.random.key(seed), 6)
    return {
        "field": normal_values(key_list[0], (BATCH, NX, NY, NZ, C), 1.0, 6.0, ((0, 32), (1, 16))),
        "cotangent": normal_values(key_list[1], (BATCH, NX, NY, NZ, C), 1.0, 6.0, ((0, 32), (1, 16))),
        "weights": normal_values(key_list[2], (MX, MYZ, 2, C, C), (2 * C) ** -0.5, 0.375, ((0, 16), (1, 32)), jnp.float32),
        "first_moment": normal_values(key_list[3], (MX, MYZ, 2, C, C), 1.0, 6.0, ((0, 16), (1, 32)), jnp.float32),
        "second_moment": jnp.clip(jnp.exp(math.log(10.0) - 6.9077553 * jax.random.uniform(key_list[4], (MX, MYZ, 2, C, C), jnp.float32) ** block_levels(key_list[4], (MX, MYZ, 2, C, C), ((0, 16), (1, 32)), -0.2, 0.2)), 0.01, 10.0),
    }


decay_first = 0.9
decay_second = 0.999
learn_rate = 0.001
adam_floor = 1e-08

def round_half(values):
    return lax.optimization_barrier(values.astype(jnp.bfloat16))

def trig_tables(length, modes_kept, signed):
    points = jnp.arange(length, dtype=jnp.int32)
    frequency = jnp.arange(modes_kept, dtype=jnp.int32) - (modes_kept // 2 if signed else 0)
    phases = jnp.mod(points[:, None] * frequency[None, :], length).astype(jnp.float32)
    angles = phases * (2.0 * math.pi / length)
    factor = 1.0 / math.sqrt(length)
    return ((jnp.cos(angles) * factor).astype(jnp.bfloat16), (jnp.sin(angles) * factor).astype(jnp.bfloat16))

def forward_table(cosine, sine_part):
    real_row = jnp.stack([cosine, -sine_part], axis=-1)
    imag_row = jnp.stack([sine_part, cosine], axis=-1)
    return jnp.stack([real_row, imag_row], axis=1)

def inverse_table(cosine, sine_part):
    real_row = jnp.stack([cosine.T, sine_part.T], axis=-1)
    imag_row = jnp.stack([-sine_part.T, cosine.T], axis=-1)
    return jnp.stack([real_row, imag_row], axis=1)

def adam_update(weights, first_moment, second_moment, weight_grads):
    new_first = decay_first * first_moment + (1.0 - decay_first) * weight_grads
    new_second = decay_second * second_moment + (1.0 - decay_second) * weight_grads * weight_grads
    first_hat = new_first / (1.0 - decay_first ** STEP)
    second_hat = new_second / (1.0 - decay_second ** STEP)
    new_weights = weights - learn_rate * first_hat / (jnp.sqrt(second_hat) + adam_floor)
    return (new_weights, new_first, new_second)

def reference(field, cotangent, weights, first_moment, second_moment):
    f32 = jnp.float32
    cos_z, sin_z = trig_tables(NZ, MZ, False)
    cos_y, sin_y = trig_tables(NY, MY, True)
    cos_x, sin_x = trig_tables(NX, MX, True)
    table_z = jnp.stack([cos_z, -sin_z], axis=1).astype(f32)
    table_y = forward_table(cos_y, sin_y).astype(f32)
    table_x = forward_table(cos_x, sin_x).astype(f32)
    back_table_x = inverse_table(cos_x, sin_x).astype(f32)
    back_table_y = inverse_table(cos_y, sin_y).astype(f32)
    back_table_z = jnp.stack([cos_z.T, -sin_z.T], axis=0).astype(f32)

    def to_modes(sample):
        first_pass = round_half(jnp.einsum('xyzc,zpk->xypkc', sample.astype(f32), table_z))
        second = round_half(jnp.einsum('xypkc,ypmq->xmkqc', first_pass.astype(f32), table_y))
        second = second.reshape(NX, MY * MZ, 2, C)
        return round_half(jnp.einsum('xpjc,xjmq->mpqc', second.astype(f32), table_x))
    field_hat = lax.map(to_modes, field).astype(f32)
    cot_hat = lax.map(to_modes, cotangent).astype(f32)
    rotated = jnp.stack([cot_hat[..., 1, :], -cot_hat[..., 0, :]], axis=-2)
    grad_real = jnp.einsum('bmpjc,bmpjo->mpco', field_hat, cot_hat)
    grad_imag = jnp.einsum('bmpjc,bmpjo->mpco', field_hat, rotated)
    weight_grads = jnp.stack([grad_real, grad_imag], axis=2)
    half_weights = round_half(weights).astype(f32)
    back_real = jnp.einsum('mpjio,bmpjo->bmpi', half_weights, cot_hat)
    back_imag = jnp.einsum('mpjio,bmpjo->bmpi', half_weights, rotated)
    mode_grads = round_half(jnp.stack([back_real, back_imag], axis=3))

    def to_field(sample_modes):
        back_x = round_half(jnp.einsum('mpjc,mjxq->xpqc', sample_modes.astype(f32), back_table_x))
        back_x = back_x.reshape(NX, MY, MZ, 2, C)
        back_y = round_half(jnp.einsum('xmkjc,mjyq->xyqkc', back_x.astype(f32), back_table_y))
        return jnp.einsum('xyqkc,qkz->xyzc', back_y.astype(f32), back_table_z).astype(jnp.bfloat16)
    field_grad = lax.map(to_field, mode_grads)
    new_weights, new_first, new_second = adam_update(weights, first_moment, second_moment, weight_grads)
    return (field_grad, new_weights, new_first, new_second)
```

```python
import functools

import jax
import jax.numpy as jnp
import numpy as np
from jax import lax
from jax.experimental import pallas as pl
from jax.experimental.pallas import tpu as pltpu
from jax.sharding import PartitionSpec as P
import ml_dtypes

C = 128
MX = 16
MY = 16
MZ = 8
NX = 64
NY = 32
NZ = 16
STEP = 100
MYZ = 128

decay_first = 0.9
decay_second = 0.999
learn_rate = 0.001
adam_floor = 1e-08

MESH = pl.DeviceIdType.MESH
BF16 = jnp.bfloat16
F32 = jnp.float32


def trig_tables(length, modes_kept, signed):
    points = np.arange(length)
    frequency = np.arange(modes_kept) - (modes_kept // 2 if signed else 0)
    phases = np.mod(points[:, None] * frequency[None, :], length).astype(np.float32)
    angles = (phases * np.float32(2.0 * np.pi / length)).astype(np.float32)
    factor = np.float32(1.0 / np.sqrt(length))
    cos_t = (np.cos(angles) * factor).astype(ml_dtypes.bfloat16).astype(np.float32)
    sin_t = (np.sin(angles) * factor).astype(ml_dtypes.bfloat16).astype(np.float32)
    return cos_t, sin_t


def complex_rows(re, im):
    return np.stack([np.stack([re, -im], axis=-1), np.stack([im, re], axis=-1)], axis=1)


@functools.cache
def tables():
    cos_z, sin_z = trig_tables(NZ, MZ, False)
    cos_y, sin_y = trig_tables(NY, MY, True)
    cos_x, sin_x = trig_tables(NX, MX, True)
    ez = cos_z - 1j * sin_z
    ey = cos_y - 1j * sin_y
    ex = cos_x - 1j * sin_x
    yz = np.einsum("ym,zk->mkyz", ey, ez)
    yz = np.stack([yz.real, yz.imag], axis=2).reshape(MYZ * 2, NY * NZ)
    zy = np.einsum("ym,zk->yzmk", ey.conj(), ez.conj())
    zy = np.stack([zy.real, -zy.imag], axis=4).reshape(NY * NZ, MYZ * 2)
    eye = np.eye(8)
    fx = complex_rows(ex.T.real, ex.T.imag)
    fx = np.einsum("msxr,pq->mpsxqr", fx, eye).reshape(MX * 16, NX * 16)
    bx = complex_rows(ex.conj().real, ex.conj().imag)
    bx = np.einsum("xsmr,pq->xpsmqr", bx, eye).reshape(NX * 16, MX * 16)
    return tuple(t.astype(ml_dtypes.bfloat16) for t in (yz, fx, bx, zy))


def tri(v):
    return lax.rem(v * (v + 1) // 2, 4)


def dot(a, b):
    return jnp.dot(a, b, preferred_element_type=F32)


def kernel(
    field_hbm,
    cot_hbm,
    w_hbm,
    yz_hbm,
    fx_hbm,
    bx_hbm,
    modes_hbm,
    grads_hbm,
    cot_v,
    field_v,
    w_v,
    yz_v,
    fx_v,
    bx_v,
    half_v,
    send1,
    recv1,
    send2,
    recv2,
    big_g,
    send3,
    recv3,
    send4,
    grads_v,
    in_sem,
    out_sem,
    send_sem,
    recv_sem,
):
    dp = lax.axis_index("dp")
    sp = lax.axis_index("space")
    gx, gz, core = dp // 8, lax.rem(dp // 2, 4), lax.rem(dp, 2)
    sy, sz = sp // 4, lax.rem(sp, 4)
    mine = dp // 2

    def block_of(x, zh, c, s):
        y, zl = s // 4, lax.rem(s, 4)
        bx_ = lax.rem(x + y + 2 * c, 4)
        bz_ = lax.rem(zh + 3 + (1 + 2 * c) * tri(zl), 4)
        return bx_ * 4 + bz_

    def space_of(x, zh, c, q):
        bx_, bz_ = q // 4, lax.rem(q, 4)
        y = lax.rem(bx_ - x - 2 * c + 8, 4)
        zl = tri(lax.rem((1 + 2 * c) * (bz_ - zh + 5), 4))
        return y * 4 + zl

    my_block = block_of(gx, gz, core, sp)
    self_in = my_block == mine

    def load(k, src, dst):
        copy = pltpu.make_async_copy(src, dst, in_sem.at[k])
        copy.start()
        return copy

    loads = [
        load(0, yz_hbm, yz_v),
        load(1, cot_hbm, cot_v),
        load(2, field_hbm, field_v),
        load(3, fx_hbm, fx_v),
        load(4, w_hbm, w_v),
        load(5, bx_hbm, bx_v),
    ]

    barrier = pltpu.get_barrier_semaphore()

    @pl.loop(0, 16)
    def _(k):
        @pl.when(k != sp)
        def _():
            pl.semaphore_signal(barrier, inc=1, device_id=(dp, k), device_id_type=MESH)

    @pl.loop(0, 32)
    def _(b):
        s = space_of(b // 8, lax.rem(b // 2, 4), lax.rem(b, 2), mine)

        @pl.when(jnp.logical_not(jnp.logical_and(b == dp, s == sp)))
        def _():
            pl.semaphore_signal(barrier, inc=1, device_id=(b, s), device_id_type=MESH)

        there = (2 * my_block + lax.rem(b, 2), b // 2)

        @pl.when(jnp.logical_not(jnp.logical_and(there[0] == dp, there[1] == sp)))
        def _():
            pl.semaphore_signal(barrier, inc=1, device_id=there, device_id_type=MESH)

    def copy_to(src, dst, stage, device):
        same = jnp.logical_and(device[0] == dp, device[1] == sp)

        @pl.when(same)
        def _():
            pltpu.make_async_copy(src, dst, recv_sem.at[stage]).start()

        @pl.when(jnp.logical_not(same))
        def _():
            pltpu.make_async_remote_copy(
                src_ref=src,
                dst_ref=dst,
                send_sem=send_sem.at[stage],
                recv_sem=recv_sem.at[stage],
                device_id=device,
                device_id_type=MESH,
            ).start()

    def yz_modes(k, slab):
        for x in range(4):
            out = dot(yz_v[...], slab[x])
            send1[k, :, x] = out.astype(BF16).reshape(16, 16, C)

    def send_slab(k):
        @pl.loop(0, 16)
        def _(q):
            there = (dp, space_of(gx, gz, core, q))
            copy_to(send1.at[k, q], recv1.at[k, sp], k, there)

    def arrived(buf, stage):
        pltpu.make_async_copy(buf, buf, recv_sem.at[stage]).wait()

    def x_modes(k):
        out = dot(fx_v[...], recv1[k].reshape(1024, C))
        send2[k] = out.astype(BF16).reshape(32, 8, C)

        @pl.loop(0, 32)
        def _(m):
            there = (2 * my_block + lax.rem(m, 2), m // 2)
            copy_to(send2.at[k, m], recv2.at[k, dp], 2 + k, there)

    loads[0].wait()
    loads[1].wait()
    yz_modes(0, cot_v)

    @pl.when(self_in)
    def _():
        pl.semaphore_wait(barrier, 15 + 62)

    @pl.when(jnp.logical_not(self_in))
    def _():
        pl.semaphore_wait(barrier, 15 + 64)

    send_slab(0)
    loads[2].wait()
    yz_modes(1, field_v)
    send_slab(1)
    loads[3].wait()
    loads[4].wait()
    half_v[...] = w_v[...].astype(BF16)

    arrived(recv1.at[0], 0)
    x_modes(0)
    arrived(recv1.at[1], 1)
    x_modes(1)

    arrived(recv2.at[0], 2)
    cot = recv2[0].astype(F32).reshape(256, C)
    row = lax.broadcasted_iota(jnp.int32, (256, C), 0)
    turned = jnp.where(
        lax.rem(row, 2) == 0, pltpu.roll(cot, 255, 0), -pltpu.roll(cot, 1, 0)
    )
    pencil = lax.rem(row // 2, 4)
    back = jnp.zeros((256, C), F32)
    for j in range(4):
        for part, rows in ((0, cot), (1, turned)):
            g = jnp.where(pencil == j, rows, 0.0).astype(BF16)
            big_g[:, pl.ds((2 * j + part) * C, C)] = g
            back += lax.dot_general(
                g, half_v[2 * j + part], (((1,), (1,)), ((), ())), preferred_element_type=F32
            )
    send3[...] = back.astype(BF16).reshape(32, 8, C)

    @pl.loop(0, 32)
    def _(b):
        there = (b, space_of(b // 8, lax.rem(b // 2, 4), lax.rem(b, 2), mine))
        copy_to(send3.at[b], recv3.at[sp, core], 4, there)

    arrived(recv2.at[1], 3)
    left = recv2[1].astype(F32).reshape(256, C).T.astype(BF16)
    for n in range(8):
        grads_v[n] = dot(left, big_g[:, pl.ds(n * C, C)])
    out = pltpu.make_async_copy(grads_v, grads_hbm, out_sem)
    out.start()

    loads[5].wait()
    arrived(recv3, 4)
    out4 = dot(bx_v[...], recv3[...].astype(F32).reshape(256, C).astype(BF16))
    send4[...] = out4.astype(BF16).reshape(16, 4, 16, C)

    @pl.loop(0, 16)
    def _(s):
        copy_to(send4.at[s], modes_hbm.at[my_block], 5, (dp, s))

    arrived(modes_hbm, 5)
    out.wait()

    def sent(buf, stage):
        pltpu.make_async_copy(buf, buf, send_sem.at[stage]).wait()

    for k in range(2):
        sent(send1.at[k, pl.ds(0, 15)], k)
    sent(send4.at[pl.ds(0, 15)], 5)

    @pl.when(self_in)
    def _():
        for k in range(2):
            sent(send2.at[k, pl.ds(0, 31)], 2 + k)
        sent(send3.at[pl.ds(0, 31)], 4)

    @pl.when(jnp.logical_not(self_in))
    def _():
        for k in range(2):
            sent(send2.at[k], 2 + k)
        sent(send3, 4)


def exchange(field, cot, weights, yz, fx, bx):
    any_spec = pl.BlockSpec(memory_space=pl.ANY)
    return pl.pallas_call(
        kernel,
        out_shape=(
            jax.ShapeDtypeStruct((16, 4, 16, C), BF16),
            jax.ShapeDtypeStruct((8, C, C), F32),
        ),
        in_specs=[any_spec] * 6,
        out_specs=(any_spec, any_spec),
        scratch_shapes=[
            pltpu.VMEM((4, 512, C), BF16),
            pltpu.VMEM((4, 512, C), BF16),
            pltpu.VMEM((8, C, C), F32),
            pltpu.VMEM((256, 512), BF16),
            pltpu.VMEM((256, 1024), BF16),
            pltpu.VMEM((1024, 256), BF16),
            pltpu.VMEM((8, C, C), BF16),
            pltpu.VMEM((2, 16, 4, 16, C), BF16),
            pltpu.VMEM((2, 16, 4, 16, C), BF16),
            pltpu.VMEM((2, 32, 8, C), BF16),
            pltpu.VMEM((2, 32, 8, C), BF16),
            pltpu.VMEM((256, 1024), BF16),
            pltpu.VMEM((32, 8, C), BF16),
            pltpu.VMEM((16, 2, 8, C), BF16),
            pltpu.VMEM((16, 4, 16, C), BF16),
            pltpu.VMEM((8, C, C), F32),
            pltpu.SemaphoreType.DMA((6,)),
            pltpu.SemaphoreType.DMA,
            pltpu.SemaphoreType.DMA((6,)),
            pltpu.SemaphoreType.DMA((6,)),
        ],
        compiler_params=pltpu.CompilerParams(collective_id=0, has_side_effects=True),
    )(field, cot, weights, yz, fx, bx)


def adam_update(weights, first_moment, second_moment, weight_grads):
    new_first = decay_first * first_moment + (1.0 - decay_first) * weight_grads
    new_second = decay_second * second_moment + (1.0 - decay_second) * weight_grads * weight_grads
    first_hat = new_first / (1.0 - decay_first**STEP)
    second_hat = new_second / (1.0 - decay_second**STEP)
    new_weights = weights - learn_rate * first_hat / (jnp.sqrt(second_hat) + adam_floor)
    return (new_weights, new_first, new_second)


def on_device(field, cotangent, weights, first_moment, second_moment):
    yz, fx, bx, zy = (jnp.asarray(t) for t in tables())
    modes, grads = exchange(
        field.reshape(4, 512, C),
        cotangent.reshape(4, 512, C),
        weights.reshape(8, C, C),
        yz,
        fx,
        bx,
    )
    field_grad = jnp.einsum(
        "nk,xkc->xnc",
        zy,
        modes.transpose(1, 0, 2, 3).reshape(4, 256, C),
        preferred_element_type=F32,
    ).astype(BF16)
    new_weights, new_first, new_second = adam_update(
        weights, first_moment, second_moment, grads.reshape(weights.shape)
    )
    return (field_grad.reshape(field.shape), new_weights, new_first, new_second)


def solution(mesh):
    placed = (
        P("dp", "space", None, None, None),
        P("dp", "space", None, None, None),
        P("space", "dp", None, None, None),
        P("space", "dp", None, None, None),
        P("space", "dp", None, None, None),
    )
    return jax.shard_map(
        on_device,
        mesh=mesh,
        in_specs=placed,
        out_specs=(
            P("dp", "space", None, None, None),
            P("space", "dp", None, None, None),
            P("space", "dp", None, None, None),
            P("space", "dp", None, None, None),
        ),
        check_vma=False,
    )
```

```python
import functools

import jax
import jax.numpy as jnp
import numpy as np
from jax import lax
from jax.experimental import pallas as pl
from jax.experimental.pallas import tpu as pltpu
from jax.sharding import PartitionSpec as P
import ml_dtypes

C = 128
MX = 16
MY = 16
MZ = 8
NX = 64
NY = 32
NZ = 16
STEP = 100
MYZ = 128

decay_first = 0.9
decay_second = 0.999
learn_rate = 0.001
adam_floor = 1e-08

VMEM_GRANT = 64 * 2**20 - 2240 * 1024

MESH = pl.DeviceIdType.MESH
BF16 = jnp.bfloat16
F32 = jnp.float32


def trig_tables(length, modes_kept, signed):
    points = np.arange(length)
    frequency = np.arange(modes_kept) - (modes_kept // 2 if signed else 0)
    phases = np.mod(points[:, None] * frequency[None, :], length).astype(np.float32)
    angles = (phases * np.float32(2.0 * np.pi / length)).astype(np.float32)
    factor = np.float32(1.0 / np.sqrt(length))
    cos_t = (np.cos(angles) * factor).astype(ml_dtypes.bfloat16).astype(np.float32)
    sin_t = (np.sin(angles) * factor).astype(ml_dtypes.bfloat16).astype(np.float32)
    return cos_t, sin_t


def complex_rows(re, im):
    return np.stack([np.stack([re, -im], axis=-1), np.stack([im, re], axis=-1)], axis=1)


@functools.cache
def tables():
    cos_z, sin_z = trig_tables(NZ, MZ, False)
    cos_y, sin_y = trig_tables(NY, MY, True)
    cos_x, sin_x = trig_tables(NX, MX, True)
    ez = cos_z - 1j * sin_z
    ey = cos_y - 1j * sin_y
    ex = cos_x - 1j * sin_x
    yz = np.einsum("ym,zk->mkyz", ey, ez)
    yz = np.stack([yz.real, yz.imag], axis=2).reshape(MYZ * 2, NY * NZ)
    zy = np.einsum("ym,zk->yzmk", ey.conj(), ez.conj())
    zy = np.stack([zy.real, -zy.imag], axis=4).reshape(NY * NZ, MYZ * 2)
    eye = np.eye(8)
    fx = complex_rows(ex.T.real, ex.T.imag)
    fx = np.einsum("msxr,pq->mpsxqr", fx, eye).reshape(MX * 16, NX * 16)
    bx = complex_rows(ex.conj().real, ex.conj().imag)
    bx = np.einsum("xsmr,pq->xpsmqr", bx, eye).reshape(NX * 16, MX * 16)
    return tuple(t.astype(ml_dtypes.bfloat16) for t in (yz, fx, bx, zy))


def tri(v):
    return lax.rem(v * (v + 1) // 2, 4)


def dot(a, b):
    return jnp.dot(a, b, preferred_element_type=F32)


def kernel(
    field_hbm,
    cot_hbm,
    w_hbm,
    first_hbm,
    second_hbm,
    yz_hbm,
    fx_hbm,
    bx_hbm,
    modes,
    new_w,
    new_first,
    new_second,
    cot_v,
    field_v,
    w_v,
    first_v,
    second_v,
    yz_v,
    fx_v,
    bx_v,
    half_v,
    send1,
    recv1,
    send2,
    recv2,
    big_g,
    send3,
    recv3,
    send4,
    in_sem,
    send_sem,
    recv_sem,
):
    dp = lax.axis_index("dp")
    sp = lax.axis_index("space")
    gx, gz, core = dp // 8, (dp // 2) % 4, dp % 2
    sy, sz = sp // 4, sp % 4
    mine = dp // 2
    mx, mz = mine // 4, mine % 4

    half_way = (sz + 2) % 4
    peer_z = (3 - sz, half_way, 3 - half_way, sz)
    peer_y = tuple((sy + i) % 4 for i in range(4))
    block_y = tuple(((gx + y + 2 * core) % 4) * 4 for y in peer_y)
    block_z = tuple((gz + 3 + (1 + 2 * core) * tri(z)) % 4 for z in peer_z)
    peers = [
        (peer_y[iy] * 4 + peer_z[iz], block_y[iy] + block_z[iz])
        for iz in range(4)
        for iy in (2, 1, 3, 0)
    ]
    my_block = peers[-1][1]
    self_in = my_block == mine

    holders = []
    for i in range(16):
        k = (sp + i) % 16
        for ic in range(2):
            c = (core + ic) % 2
            holders.append((2 * my_block + c, k, 2 * k + c))

    at_y, at_z, sample = {}, {}, {}
    for ic in range(2):
        c = (core + ic) % 2
        for i in range(4):
            x, z = (gx + i) % 4, (gz + i) % 4
            at_y[i, ic] = ((mx - x - 2 * c + 8) % 4) * 4
            at_z[i, ic] = tri(((1 + 2 * c) * (mz - z + 5)) % 4)
            sample["x", i] = x * 8
            sample["z", i] = z * 2
        sample["c", ic] = c
    samples = []
    for iz in (0, 2, 1, 3):
        for ix in (0, 2, 1, 3):
            for ic in range(2):
                b = sample["x", ix] + sample["z", iz] + sample["c", ic]
                samples.append((b, at_y[ix, ic] + at_z[iz, ic]))

    def load(k, src, dst):
        copy = pltpu.make_async_copy(src, dst, in_sem.at[k])
        copy.start()
        return copy

    loads = [load(0, yz_hbm, yz_v), load(1, cot_hbm, cot_v)]

    barrier = pltpu.get_barrier_semaphore()

    def hello(b, s):
        pl.semaphore_signal(barrier, inc=1, device_id=(b, s), device_id_type=MESH)

    for s, _ in peers[:-1]:
        hello(dp, s)
    for b, s in samples[1:]:
        hello(b, s)
    for b, s, _ in holders[1:]:
        hello(b, s)

    @pl.when(jnp.logical_not(self_in))
    def _():
        hello(*samples[0])
        hello(*holders[0][:2])

    loads += [
        load(2, field_hbm, field_v),
        load(3, fx_hbm, fx_v),
        load(4, w_hbm, w_v),
        load(5, bx_hbm, bx_v),
        load(6, first_hbm, first_v),
        load(7, second_hbm, second_v),
    ]

    def remote(src, dst, stage, b, s):
        pltpu.make_async_remote_copy(
            src_ref=src,
            dst_ref=dst,
            send_sem=send_sem.at[stage],
            recv_sem=recv_sem.at[stage],
            device_id=(b, s),
            device_id_type=MESH,
        ).start()

    def local(src, dst, stage):
        pltpu.make_async_copy(src, dst, recv_sem.at[stage]).start()

    def maybe_local(src, dst, stage, b, s):
        @pl.when(self_in)
        def _():
            local(src, dst, stage)

        @pl.when(jnp.logical_not(self_in))
        def _():
            remote(src, dst, stage, b, s)

    def arrived(buf, stage):
        with jax.named_scope(f"wait_recv{stage}"):
            pltpu.make_async_copy(buf, buf, recv_sem.at[stage]).wait()

    def yz_modes(k, slab):
        for x in range(4):
            out = dot(yz_v[...], slab[x])
            send1[k, :, x] = out.astype(BF16).reshape(16, 16, C)

    def send_slab(k):
        for s, q in peers[:-1]:
            remote(send1.at[k, q], recv1.at[k, sp], k, dp, s)
        local(send1.at[k, my_block], recv1.at[k, sp], k)

    def x_modes(k):
        out = dot(fx_v[...], recv1[k].reshape(1024, C))
        send2[k] = out.astype(BF16).reshape(32, 8, C)
        for b, s, m in holders[1:]:
            remote(send2.at[k, m], recv2.at[k, dp], 2 + k, b, s)
        b, s, m = holders[0]
        maybe_local(send2.at[k, m], recv2.at[k, dp], 2 + k, b, s)

    loads[0].wait()
    loads[1].wait()
    yz_modes(0, cot_v)

    with jax.named_scope("wait_barrier"):

        @pl.when(self_in)
        def _():
            pl.semaphore_wait(barrier, 15 + 62)

        @pl.when(jnp.logical_not(self_in))
        def _():
            pl.semaphore_wait(barrier, 15 + 64)

    send_slab(0)
    loads[2].wait()
    yz_modes(1, field_v)
    loads[3].wait()
    loads[4].wait()
    half_v[...] = w_v[...].astype(BF16)

    arrived(recv1.at[0], 0)
    x_modes(0)
    send_slab(1)

    arrived(recv2.at[0], 2)
    cot = recv2[0].astype(F32).reshape(256, C)
    row = lax.broadcasted_iota(jnp.int32, (256, C), 0)
    turned = jnp.where(
        lax.rem(row, 2) == 0, pltpu.roll(cot, 255, 0), -pltpu.roll(cot, 1, 0)
    )
    pencil = lax.rem(row // 2, 4)
    back = jnp.zeros((256, C), F32)
    for j in range(4):
        for part, rows in ((0, cot), (1, turned)):
            g = jnp.where(pencil == j, rows, 0.0).astype(BF16)
            big_g[:, pl.ds((2 * j + part) * C, C)] = g
            back += lax.dot_general(
                g, half_v[2 * j + part], (((1,), (1,)), ((), ())), preferred_element_type=F32
            )
    send3[...] = back.astype(BF16).reshape(32, 8, C)
    for b, s in samples[1:]:
        remote(send3.at[b], recv3.at[sp, core], 4, b, s)
    maybe_local(send3.at[dp], recv3.at[sp, core], 4, *samples[0])

    arrived(recv1.at[1], 1)
    x_modes(1)

    loads[5].wait()
    arrived(recv3, 4)
    out4 = dot(bx_v[...], recv3[...].astype(F32).reshape(256, C).astype(BF16))
    send4[...] = out4.astype(BF16).reshape(16, 4, 16, C)
    for s, _ in peers[:-1]:
        remote(send4.at[s], modes.at[my_block], 5, dp, s)
    local(send4.at[sp], modes.at[my_block], 5)

    loads[6].wait()
    loads[7].wait()
    arrived(recv2.at[1], 3)
    left = recv2[1].astype(F32).reshape(256, C).T.astype(BF16)
    for n in range(8):
        grads = dot(left, big_g[:, pl.ds(n * C, C)])
        new_w[n], new_first[n], new_second[n] = adam_update(
            w_v[n], first_v[n], second_v[n], grads
        )

    def sent(buf, stage):
        pltpu.make_async_copy(buf, buf, send_sem.at[stage]).wait()

    for k in range(2):
        sent(send1.at[k, pl.ds(0, 15)], k)

    @pl.when(self_in)
    def _():
        for k in range(2):
            sent(send2.at[k, pl.ds(0, 31)], 2 + k)
        sent(send3.at[pl.ds(0, 31)], 4)

    @pl.when(jnp.logical_not(self_in))
    def _():
        for k in range(2):
            sent(send2.at[k], 2 + k)
        sent(send3, 4)

    sent(send4.at[pl.ds(0, 15)], 5)
    arrived(modes, 5)


def exchange(field, cot, weights, first, second, yz, fx, bx):
    any_spec = pl.BlockSpec(memory_space=pl.ANY)
    vmem_spec = pl.BlockSpec(memory_space=pltpu.VMEM)
    part = pltpu.VMEM((8, C, C), F32)
    return pl.pallas_call(
        kernel,
        out_shape=(pltpu.VMEM((16, 4, 16, C), BF16), part, part, part),
        in_specs=[any_spec] * 8,
        out_specs=(vmem_spec,) * 4,
        scratch_shapes=[
            pltpu.VMEM((4, 512, C), BF16),
            pltpu.VMEM((4, 512, C), BF16),
            part,
            part,
            part,
            pltpu.VMEM((256, 512), BF16),
            pltpu.VMEM((256, 1024), BF16),
            pltpu.VMEM((1024, 256), BF16),
            pltpu.VMEM((8, C, C), BF16),
            pltpu.VMEM((2, 16, 4, 16, C), BF16),
            pltpu.VMEM((2, 16, 4, 16, C), BF16),
            pltpu.VMEM((2, 32, 8, C), BF16),
            pltpu.VMEM((2, 32, 8, C), BF16),
            pltpu.VMEM((256, 1024), BF16),
            pltpu.VMEM((32, 8, C), BF16),
            pltpu.VMEM((16, 2, 8, C), BF16),
            pltpu.VMEM((16, 4, 16, C), BF16),
            pltpu.SemaphoreType.DMA((8,)),
            pltpu.SemaphoreType.DMA((6,)),
            pltpu.SemaphoreType.DMA((6,)),
        ],
        compiler_params=pltpu.CompilerParams(
            collective_id=0, has_side_effects=True, vmem_limit_bytes=VMEM_GRANT
        ),
    )(field, cot, weights, first, second, yz, fx, bx)


def finish_kernel(
    modes, zy, new_w, new_first, new_second, grad_hbm, w_hbm, first_hbm, second_hbm, grad_v, sem
):
    copies = []

    def store(k, src, dst):
        copy = pltpu.make_async_copy(src, dst, sem.at[k])
        copy.start()
        copies.append(copy)

    store(0, new_w, w_hbm)
    store(1, new_first, first_hbm)
    store(2, new_second, second_hbm)
    for x in range(4):
        out = dot(zy[...], modes[:, x].reshape(256, C))
        grad_v[x] = out.astype(BF16)
        store(3 + x, grad_v.at[x], grad_hbm.at[x])
    for copy in copies:
        copy.wait()


def finish(modes, zy, new_w, new_first, new_second):
    any_spec = pl.BlockSpec(memory_space=pl.ANY)
    vmem_spec = pl.BlockSpec(memory_space=pltpu.VMEM)
    part = jax.ShapeDtypeStruct((8, C, C), F32)
    return pl.pallas_call(
        finish_kernel,
        out_shape=(jax.ShapeDtypeStruct((4, 512, C), BF16), part, part, part),
        in_specs=[vmem_spec] * 5,
        out_specs=(any_spec,) * 4,
        scratch_shapes=[pltpu.VMEM((4, 512, C), BF16), pltpu.SemaphoreType.DMA((7,))],
        compiler_params=pltpu.CompilerParams(vmem_limit_bytes=16 * 2**20),
    )(modes, zy, new_w, new_first, new_second)


def adam_update(weights, first_moment, second_moment, weight_grads):
    new_first = decay_first * first_moment + (1.0 - decay_first) * weight_grads
    new_second = decay_second * second_moment + (1.0 - decay_second) * weight_grads * weight_grads
    first_hat = new_first / (1.0 - decay_first**STEP)
    second_hat = new_second / (1.0 - decay_second**STEP)
    new_weights = weights - learn_rate * first_hat / (jnp.sqrt(second_hat) + adam_floor)
    return (new_weights, new_first, new_second)


def on_device(field, cotangent, weights, first_moment, second_moment):
    yz, fx, bx, zy = (jnp.asarray(t) for t in tables())
    modes, new_weights, new_first, new_second = exchange(
        field.reshape(4, 512, C),
        cotangent.reshape(4, 512, C),
        weights.reshape(8, C, C),
        first_moment.reshape(8, C, C),
        second_moment.reshape(8, C, C),
        yz,
        fx,
        bx,
    )
    field_grad, *state = finish(modes, zy, new_weights, new_first, new_second)
    return (field_grad.reshape(field.shape), *(a.reshape(weights.shape) for a in state))


def solution(mesh):
    placed = (
        P("dp", "space", None, None, None),
        P("dp", "space", None, None, None),
        P("space", "dp", None, None, None),
        P("space", "dp", None, None, None),
        P("space", "dp", None, None, None),
    )
    return jax.shard_map(
        on_device,
        mesh=mesh,
        in_specs=placed,
        out_specs=(
            P("dp", "space", None, None, None),
            P("space", "dp", None, None, None),
            P("space", "dp", None, None, None),
            P("space", "dp", None, None, None),
        ),
        check_vma=False,
    )
```

```python
import functools

import jax
import jax.numpy as jnp
import numpy as np
from jax import lax
from jax.experimental import pallas as pl
from jax.experimental.pallas import tpu as pltpu
from jax.sharding import PartitionSpec as P
import ml_dtypes

C = 128
MX = 16
MY = 16
MZ = 8
NX = 64
NY = 32
NZ = 16
STEP = 100
MYZ = 128

decay_first = 0.9
decay_second = 0.999
learn_rate = 0.001
adam_floor = 1e-08

VMEM_GRANT = 64 * 2**20 - 2240 * 1024

MESH = pl.DeviceIdType.MESH
BF16 = jnp.bfloat16
F32 = jnp.float32


def trig_tables(length, modes_kept, signed):
    points = np.arange(length)
    frequency = np.arange(modes_kept) - (modes_kept // 2 if signed else 0)
    phases = np.mod(points[:, None] * frequency[None, :], length).astype(np.float32)
    angles = (phases * np.float32(2.0 * np.pi / length)).astype(np.float32)
    factor = np.float32(1.0 / np.sqrt(length))
    cos_t = (np.cos(angles) * factor).astype(ml_dtypes.bfloat16).astype(np.float32)
    sin_t = (np.sin(angles) * factor).astype(ml_dtypes.bfloat16).astype(np.float32)
    return cos_t, sin_t


def complex_rows(re, im):
    return np.stack([np.stack([re, -im], axis=-1), np.stack([im, re], axis=-1)], axis=1)


@functools.cache
def tables():
    cos_z, sin_z = trig_tables(NZ, MZ, False)
    cos_y, sin_y = trig_tables(NY, MY, True)
    cos_x, sin_x = trig_tables(NX, MX, True)
    ez = cos_z - 1j * sin_z
    ey = cos_y - 1j * sin_y
    ex = cos_x - 1j * sin_x
    yz = np.einsum("ym,zk->mkyz", ey, ez)
    yz = np.stack([yz.real, yz.imag], axis=2).reshape(MYZ * 2, NY * NZ)
    zy = np.einsum("ym,zk->yzmk", ey.conj(), ez.conj())
    zy = np.stack([zy.real, -zy.imag], axis=4).reshape(NY * NZ, MYZ * 2)
    eye = np.eye(8)
    fx = complex_rows(ex.T.real, ex.T.imag)
    fx = np.einsum("msxr,pq->mpsxqr", fx, eye).reshape(MX * 16, NX * 16)
    bx = complex_rows(ex.conj().real, ex.conj().imag)
    bx = np.einsum("xsmr,pq->xpsmqr", bx, eye).reshape(NX * 16, MX * 16)
    return tuple(t.astype(ml_dtypes.bfloat16) for t in (yz, fx, bx, zy))


def tri(v):
    return lax.rem(v * (v + 1) // 2, 4)


def dot(a, b):
    return jnp.dot(a, b, preferred_element_type=F32)


def kernel(
    field_hbm,
    cot_hbm,
    w_hbm,
    first_hbm,
    second_hbm,
    yz_hbm,
    fx_hbm,
    bx_hbm,
    modes,
    new_w,
    new_first,
    new_second,
    cot_v,
    field_v,
    w_v,
    first_v,
    second_v,
    yz_v,
    fx_v,
    bx_v,
    half_v,
    send1,
    recv1,
    send2,
    recv2,
    big_g,
    send3,
    recv3,
    send4,
    in_sem,
    send_sem,
    recv_sem,
    met,
):
    dp = lax.axis_index("dp")
    sp = lax.axis_index("space")
    gx, gz, core = dp // 8, (dp // 2) % 4, dp % 2
    sy, sz = sp // 4, sp % 4
    mine = dp // 2
    mx, mz = mine // 4, mine % 4

    half_way = (sz + 2) % 4
    peer_z = (3 - sz, half_way, 3 - half_way, sz)
    peer_y = tuple((sy + i) % 4 for i in range(4))
    block_y = tuple(((gx + y + 2 * core) % 4) * 4 for y in peer_y)
    block_z = tuple((gz + 3 + (1 + 2 * core) * tri(z)) % 4 for z in peer_z)
    peers = [
        (peer_y[iy] * 4 + peer_z[iz], block_y[iy] + block_z[iz])
        for iz in range(4)
        for iy in (2, 1, 3, 0)
    ]
    my_block = peers[-1][1]
    self_in = my_block == mine

    holders = []
    for i in range(16):
        k = (sp + i) % 16
        for ic in range(2):
            c = (core + ic) % 2
            holders.append((2 * my_block + c, k, 2 * k + c))

    at_y, at_z, sample = {}, {}, {}
    for ic in range(2):
        c = (core + ic) % 2
        for i in range(4):
            x, z = (gx + i) % 4, (gz + i) % 4
            at_y[i, ic] = ((mx - x - 2 * c + 8) % 4) * 4
            at_z[i, ic] = tri(((1 + 2 * c) * (mz - z + 5)) % 4)
            sample["x", i] = x * 8
            sample["z", i] = z * 2
        sample["c", ic] = c
    samples = []
    for iz in (0, 2, 1, 3):
        for ix in (0, 2, 1, 3):
            for ic in range(2):
                b = sample["x", ix] + sample["z", iz] + sample["c", ic]
                samples.append((b, at_y[ix, ic] + at_z[iz, ic]))

    def load(k, src, dst):
        copy = pltpu.make_async_copy(src, dst, in_sem.at[k])
        copy.start()
        return copy

    loads = [load(0, yz_hbm, yz_v), load(1, cot_hbm, cot_v)]

    barrier = pltpu.get_barrier_semaphore()

    def hello(sem, b, s):
        pl.semaphore_signal(sem, inc=1, device_id=(b, s), device_id_type=MESH)

    plane = [
        (sample["x", ix] + gz * 2 + sample["c", ic], sp)
        for ix in range(4)
        for ic in range(2)
        if ix or ic
    ]
    beside = [(gx * 8 + sample["z", iz] + core, sp) for iz in (1, 3)]
    for s, _ in peers[:-1]:
        hello(barrier, dp, s)
    for b, s in plane + beside:
        hello(barrier, b, s)

    loads += [
        load(2, field_hbm, field_v),
        load(3, fx_hbm, fx_v),
        load(4, w_hbm, w_v),
        load(5, bx_hbm, bx_v),
        load(6, first_hbm, first_v),
        load(7, second_hbm, second_v),
    ]

    def remote(src, dst, stage, b, s):
        pltpu.make_async_remote_copy(
            src_ref=src,
            dst_ref=dst,
            send_sem=send_sem.at[stage],
            recv_sem=recv_sem.at[stage],
            device_id=(b, s),
            device_id_type=MESH,
        ).start()

    def local(src, dst, stage):
        pltpu.make_async_copy(src, dst, recv_sem.at[stage]).start()

    def maybe_local(src, dst, stage, b, s):
        @pl.when(self_in)
        def _():
            local(src, dst, stage)

        @pl.when(jnp.logical_not(self_in))
        def _():
            remote(src, dst, stage, b, s)

    def arrived(buf, stage):
        with jax.named_scope(f"wait_recv{stage}"):
            pltpu.make_async_copy(buf, buf, recv_sem.at[stage]).wait()

    def yz_modes(k, slab):
        for x in range(4):
            out = dot(yz_v[...], slab[x])
            send1[k, :, x] = out.astype(BF16).reshape(16, 16, C)

    def send_slab(k):
        for s, q in peers[:-1]:
            remote(send1.at[k, q], recv1.at[k, sp], k, dp, s)
        local(send1.at[k, my_block], recv1.at[k, sp], k)

    def x_modes(k):
        out = dot(fx_v[...], recv1[k].reshape(1024, C))
        send2[k] = out.astype(BF16).reshape(32, 8, C)
        if k == 0:
            pl.semaphore_wait(met.at[2], 2)
        for b, s, m in holders[1:]:
            remote(send2.at[k, m], recv2.at[k, dp], 2 + k, b, s)
        b, s, m = holders[0]
        maybe_local(send2.at[k, m], recv2.at[k, dp], 2 + k, b, s)

    loads[0].wait()
    loads[1].wait()
    yz_modes(0, cot_v)

    with jax.named_scope("wait_barrier"):
        pl.semaphore_wait(barrier, 15 + 7 + 2)

    send_slab(0)
    for b, s in plane:
        hello(met.at[0], b, s)
    loads[2].wait()
    yz_modes(1, field_v)
    pl.semaphore_wait(met.at[0], 7)
    for b, s in beside:
        hello(met.at[1], b, s)
    loads[3].wait()
    loads[4].wait()
    half_v[...] = w_v[...].astype(BF16)
    pl.semaphore_wait(met.at[1], 2)
    for b, s in beside:
        hello(met.at[2], b, s)

    arrived(recv1.at[0], 0)
    x_modes(0)
    send_slab(1)

    arrived(recv2.at[0], 2)
    cot = recv2[0].astype(F32).reshape(256, C)
    row = lax.broadcasted_iota(jnp.int32, (256, C), 0)
    turned = jnp.where(
        lax.rem(row, 2) == 0, pltpu.roll(cot, 255, 0), -pltpu.roll(cot, 1, 0)
    )
    pencil = lax.rem(row // 2, 4)
    back = jnp.zeros((256, C), F32)
    for j in range(4):
        for part, rows in ((0, cot), (1, turned)):
            g = jnp.where(pencil == j, rows, 0.0).astype(BF16)
            big_g[:, pl.ds((2 * j + part) * C, C)] = g
            back += lax.dot_general(
                g, half_v[2 * j + part], (((1,), (1,)), ((), ())), preferred_element_type=F32
            )
    send3[...] = back.astype(BF16).reshape(32, 8, C)
    for b, s in samples[1:]:
        remote(send3.at[b], recv3.at[sp, core], 4, b, s)
    maybe_local(send3.at[dp], recv3.at[sp, core], 4, *samples[0])

    arrived(recv1.at[1], 1)
    x_modes(1)

    loads[5].wait()
    arrived(recv3, 4)
    out4 = dot(bx_v[...], recv3[...].astype(F32).reshape(256, C).astype(BF16))
    send4[...] = out4.astype(BF16).reshape(16, 4, 16, C)
    for s, _ in peers[:-1]:
        remote(send4.at[s], modes.at[my_block], 5, dp, s)
    local(send4.at[sp], modes.at[my_block], 5)

    loads[6].wait()
    loads[7].wait()
    arrived(recv2.at[1], 3)
    left = recv2[1].astype(F32).reshape(256, C).T.astype(BF16)
    for n in range(8):
        grads = dot(left, big_g[:, pl.ds(n * C, C)])
        new_w[n], new_first[n], new_second[n] = adam_update(
            w_v[n], first_v[n], second_v[n], grads
        )

    def sent(buf, stage):
        pltpu.make_async_copy(buf, buf, send_sem.at[stage]).wait()

    for k in range(2):
        sent(send1.at[k, pl.ds(0, 15)], k)

    @pl.when(self_in)
    def _():
        for k in range(2):
            sent(send2.at[k, pl.ds(0, 31)], 2 + k)
        sent(send3.at[pl.ds(0, 31)], 4)

    @pl.when(jnp.logical_not(self_in))
    def _():
        for k in range(2):
            sent(send2.at[k], 2 + k)
        sent(send3, 4)

    sent(send4.at[pl.ds(0, 15)], 5)
    arrived(modes, 5)


def exchange(field, cot, weights, first, second, yz, fx, bx):
    any_spec = pl.BlockSpec(memory_space=pl.ANY)
    vmem_spec = pl.BlockSpec(memory_space=pltpu.VMEM)
    part = pltpu.VMEM((8, C, C), F32)
    return pl.pallas_call(
        kernel,
        out_shape=(pltpu.VMEM((16, 4, 16, C), BF16), part, part, part),
        in_specs=[any_spec] * 8,
        out_specs=(vmem_spec,) * 4,
        scratch_shapes=[
            pltpu.VMEM((4, 512, C), BF16),
            pltpu.VMEM((4, 512, C), BF16),
            part,
            part,
            part,
            pltpu.VMEM((256, 512), BF16),
            pltpu.VMEM((256, 1024), BF16),
            pltpu.VMEM((1024, 256), BF16),
            pltpu.VMEM((8, C, C), BF16),
            pltpu.VMEM((2, 16, 4, 16, C), BF16),
            pltpu.VMEM((2, 16, 4, 16, C), BF16),
            pltpu.VMEM((2, 32, 8, C), BF16),
            pltpu.VMEM((2, 32, 8, C), BF16),
            pltpu.VMEM((256, 1024), BF16),
            pltpu.VMEM((32, 8, C), BF16),
            pltpu.VMEM((16, 2, 8, C), BF16),
            pltpu.VMEM((16, 4, 16, C), BF16),
            pltpu.SemaphoreType.DMA((8,)),
            pltpu.SemaphoreType.DMA((6,)),
            pltpu.SemaphoreType.DMA((6,)),
            pltpu.SemaphoreType.REGULAR((3,)),
        ],
        compiler_params=pltpu.CompilerParams(
            collective_id=0, has_side_effects=True, vmem_limit_bytes=VMEM_GRANT
        ),
    )(field, cot, weights, first, second, yz, fx, bx)


def finish_kernel(
    modes, zy, new_w, new_first, new_second, grad_hbm, w_hbm, first_hbm, second_hbm, grad_v, sem
):
    copies = []

    def store(k, src, dst):
        copy = pltpu.make_async_copy(src, dst, sem.at[k])
        copy.start()
        copies.append(copy)

    store(0, new_w, w_hbm)
    store(1, new_first, first_hbm)
    store(2, new_second, second_hbm)
    for x in range(4):
        out = dot(zy[...], modes[:, x].reshape(256, C))
        grad_v[x] = out.astype(BF16)
        store(3 + x, grad_v.at[x], grad_hbm.at[x])
    for copy in copies:
        copy.wait()


def finish(modes, zy, new_w, new_first, new_second):
    any_spec = pl.BlockSpec(memory_space=pl.ANY)
    vmem_spec = pl.BlockSpec(memory_space=pltpu.VMEM)
    part = jax.ShapeDtypeStruct((8, C, C), F32)
    return pl.pallas_call(
        finish_kernel,
        out_shape=(jax.ShapeDtypeStruct((4, 512, C), BF16), part, part, part),
        in_specs=[vmem_spec] * 5,
        out_specs=(any_spec,) * 4,
        scratch_shapes=[pltpu.VMEM((4, 512, C), BF16), pltpu.SemaphoreType.DMA((7,))],
        compiler_params=pltpu.CompilerParams(vmem_limit_bytes=16 * 2**20),
    )(modes, zy, new_w, new_first, new_second)


def adam_update(weights, first_moment, second_moment, weight_grads):
    new_first = decay_first * first_moment + (1.0 - decay_first) * weight_grads
    new_second = decay_second * second_moment + (1.0 - decay_second) * weight_grads * weight_grads
    first_hat = new_first / (1.0 - decay_first**STEP)
    second_hat = new_second / (1.0 - decay_second**STEP)
    new_weights = weights - learn_rate * first_hat / (jnp.sqrt(second_hat) + adam_floor)
    return (new_weights, new_first, new_second)


def on_device(field, cotangent, weights, first_moment, second_moment):
    yz, fx, bx, zy = (jnp.asarray(t) for t in tables())
    modes, new_weights, new_first, new_second = exchange(
        field.reshape(4, 512, C),
        cotangent.reshape(4, 512, C),
        weights.reshape(8, C, C),
        first_moment.reshape(8, C, C),
        second_moment.reshape(8, C, C),
        yz,
        fx,
        bx,
    )
    field_grad, *state = finish(modes, zy, new_weights, new_first, new_second)
    return (field_grad.reshape(field.shape), *(a.reshape(weights.shape) for a in state))


def solution(mesh):
    placed = (
        P("dp", "space", None, None, None),
        P("dp", "space", None, None, None),
        P("space", "dp", None, None, None),
        P("space", "dp", None, None, None),
        P("space", "dp", None, None, None),
    )
    return jax.shard_map(
        on_device,
        mesh=mesh,
        in_specs=placed,
        out_specs=(
            P("dp", "space", None, None, None),
            P("space", "dp", None, None, None),
            P("space", "dp", None, None, None),
            P("space", "dp", None, None, None),
        ),
        check_vma=False,
    )
```

```python
import functools

import jax
import jax.numpy as jnp
import numpy as np
from jax import lax
from jax.experimental import pallas as pl
from jax.experimental.pallas import tpu as pltpu
from jax.sharding import PartitionSpec as P
import ml_dtypes

C = 128
MX = 16
MY = 16
MZ = 8
NX = 64
NY = 32
NZ = 16
STEP = 100
MYZ = 128

decay_first = 0.9
decay_second = 0.999
learn_rate = 0.001
adam_floor = 1e-08

VMEM_GRANT = 64 * 2**20 - 2240 * 1024

MESH = pl.DeviceIdType.MESH
BF16 = jnp.bfloat16
F32 = jnp.float32


def trig_tables(length, modes_kept, signed):
    points = np.arange(length)
    frequency = np.arange(modes_kept) - (modes_kept // 2 if signed else 0)
    phases = np.mod(points[:, None] * frequency[None, :], length).astype(np.float32)
    angles = (phases * np.float32(2.0 * np.pi / length)).astype(np.float32)
    factor = np.float32(1.0 / np.sqrt(length))
    cos_t = (np.cos(angles) * factor).astype(ml_dtypes.bfloat16).astype(np.float32)
    sin_t = (np.sin(angles) * factor).astype(ml_dtypes.bfloat16).astype(np.float32)
    return cos_t, sin_t


def complex_rows(re, im):
    return np.stack([np.stack([re, -im], axis=-1), np.stack([im, re], axis=-1)], axis=1)


@functools.cache
def tables():
    cos_z, sin_z = trig_tables(NZ, MZ, False)
    cos_y, sin_y = trig_tables(NY, MY, True)
    cos_x, sin_x = trig_tables(NX, MX, True)
    ez = cos_z - 1j * sin_z
    ey = cos_y - 1j * sin_y
    ex = cos_x - 1j * sin_x
    yz = np.einsum("ym,zk->mkyz", ey, ez)
    yz = np.stack([yz.real, yz.imag], axis=2).reshape(16, 2, 8, NY * NZ)
    yz = yz.transpose(1, 0, 2, 3).reshape(MYZ * 2, NY * NZ)
    zy = np.einsum("ym,zk->yzmk", ey.conj(), ez.conj())
    zy = np.stack([zy.real, -zy.imag], axis=4).reshape(NY * NZ, 16, 2, 8)
    zy = zy.transpose(0, 2, 1, 3).reshape(NY * NZ, MYZ * 2)
    eye = np.eye(4)
    fx = complex_rows(ex.T.real, ex.T.imag)
    fx = np.einsum("msxr,pq->mpsxqr", fx, eye).reshape(MX * 8, NX * 8)
    bx = complex_rows(ex.conj().real, ex.conj().imag)
    bx = np.einsum("xsmr,pq->xpsmqr", bx, eye).reshape(NX * 8, MX * 8)
    return tuple(t.astype(ml_dtypes.bfloat16) for t in (yz, fx, bx, zy))


def tri(v):
    return ((v * (v + 1)) >> 1) & 3


def dot(a, b):
    return jnp.dot(a, b, preferred_element_type=F32)


def kernel(
    field_hbm,
    cot_hbm,
    w_hbm,
    first_hbm,
    second_hbm,
    yz_hbm,
    fx_hbm,
    bx_hbm,
    modes,
    new_w,
    new_first,
    new_second,
    cot_v,
    field_v,
    w_v,
    first_v,
    second_v,
    yz_v,
    fx_v,
    bx_v,
    half_v,
    send1,
    recv1,
    send2,
    recv2,
    big_g,
    send3,
    recv3,
    send4,
    in_sem,
    send_sem,
    recv_sem,
    met,
):
    dp = lax.axis_index("dp")
    sp = lax.axis_index("space")

    def load(k, src, dst):
        copy = pltpu.make_async_copy(src, dst, in_sem.at[k])
        copy.start()
        return copy

    loads = [load(0, yz_hbm, yz_v), load(1, cot_hbm, cot_v)]

    def hello(sem, b, s):
        pl.semaphore_signal(sem, inc=1, device_id=(b, s), device_id_type=MESH)

    barrier = pltpu.get_barrier_semaphore()
    level = dp & 6
    plane = [level + 8 * x + c for x in range(4) for c in range(2)]
    beside = [dp - level + ((dp + 2) & 6), dp - level + ((dp + 6) & 6)]

    def hello_plane(sem):
        for b in plane:

            @pl.when(b != dp)
            def _():
                hello(sem, b, sp)

    for k in range(16):

        @pl.when(sp != k)
        def _():
            hello(barrier, dp, k)

    hello_plane(barrier)
    for b in beside:
        hello(barrier, b, sp)

    loads += [
        load(2, field_hbm, field_v),
        load(3, fx_hbm, fx_v),
        load(4, w_hbm, w_v),
        load(5, bx_hbm, bx_v),
        load(6, first_hbm, first_v),
        load(7, second_hbm, second_v),
    ]

    gx, gz, core = dp >> 3, (dp >> 1) & 3, dp & 1
    sy, sz = sp >> 2, sp & 3
    mine = dp >> 1
    mx, mz = mine >> 2, mine & 3

    half_way = (sz + 2) & 3
    peer_z = (3 - sz, half_way, 3 - half_way, sz)
    peer_y = tuple((sy + i) & 3 for i in range(4))
    block_y = tuple(((gx + y + 2 * core) & 3) * 4 for y in peer_y)
    block_z = tuple((gz + 3 + (1 + 2 * core) * tri(z)) & 3 for z in peer_z)
    peers = [
        (peer_y[iy] * 4 + peer_z[iz], block_y[iy] + block_z[iz])
        for iz in range(4)
        for iy in (2, 1, 3, 0)
    ]
    my_block = peers[-1][1]
    self_in = my_block == mine
    far_block = ((block_z[3] - gz) & 3) == 2

    at_y, at_z, sample = {}, {}, {}
    for ic in range(2):
        c = (core + ic) & 1
        for i in range(4):
            x, z = (gx + i) & 3, (gz + i) & 3
            at_y[i, ic] = ((mx - x - 2 * c + 8) & 3) * 4
            at_z[i, ic] = tri(((1 + 2 * c) * (mz - z + 5)) & 3)
            sample["x", i] = x * 8
            sample["z", i] = z * 2
        sample["c", ic] = c
    samples = []
    for iz in (0, 2, 1, 3):
        for ix in (0, 2, 1, 3):
            for ic in range(2):
                b = sample["x", ix] + sample["z", iz] + sample["c", ic]
                samples.append((b, at_y[ix, ic] + at_z[iz, ic]))

    def remote(src, dst, send, recv, b, s):
        pltpu.make_async_remote_copy(
            src_ref=src,
            dst_ref=dst,
            send_sem=send_sem.at[send],
            recv_sem=recv_sem.at[recv],
            device_id=(b, s),
            device_id_type=MESH,
        ).start()

    def local(src, dst, recv):
        pltpu.make_async_copy(src, dst, recv_sem.at[recv]).start()

    def maybe_local(here, src, dst, send, recv, b, s):
        @pl.when(here)
        def _():
            local(src, dst, recv)

        @pl.when(jnp.logical_not(here))
        def _():
            remote(src, dst, send, recv, b, s)

    def arrived(buf, stage):
        with jax.named_scope(f"wait_recv{stage}"):
            pltpu.make_async_copy(buf, buf, recv_sem.at[stage]).wait()

    def yz_modes(k, slab):
        for x in range(4):
            out = dot(yz_v[...], slab[x])
            send1[k, :, x] = out.astype(BF16).reshape(32, 8, C)

    def send_slab(k, c, stage):
        for s, q in peers[:-1]:
            remote(send1.at[k, 16 * c + q], recv1.at[k, 16 * c + sp], stage, stage, dp, s)
        local(send1.at[k, 16 * c + my_block], recv1.at[k, 16 * c + sp], stage)

    def x_modes(k, c):
        slab = recv1[k, pl.ds(16 * c, 16)].reshape(512, C)
        send2[k, pl.ds(16 * c, 16)] = dot(fx_v[...], slab).astype(BF16).reshape(16, 8, C)

    def send_modes(k, c):
        b = 2 * my_block + c
        for i in range(1, 16):
            s = (sp + i) & 15
            remote(send2.at[k, 16 * c + s], recv2.at[k, dp], 3 + k, 3 + k, b, s)
        here = jnp.logical_and(self_in, core == c)
        maybe_local(here, send2.at[k, 16 * c + sp], recv2.at[k, dp], 3 + k, 3 + k, b, sp)

    loads[0].wait()
    loads[1].wait()
    yz_modes(0, cot_v)

    with jax.named_scope("wait_barrier"):
        pl.semaphore_wait(barrier, 15 + 7 + 2)

    send_slab(0, 0, 0)
    hello_plane(met.at[0])
    send_slab(0, 1, 1)
    loads[2].wait()
    yz_modes(1, field_v)
    pl.semaphore_wait(met.at[0], 7)
    for b in beside:
        hello(met.at[1], b, sp)
    loads[3].wait()
    loads[4].wait()
    half_v[...] = w_v[...].astype(BF16)
    pl.semaphore_wait(met.at[1], 2)
    for b in beside:
        hello(met.at[2], b, sp)

    arrived(recv1.at[0, pl.ds(0, 16)], 0)
    x_modes(0, 0)

    @pl.when(far_block)
    def _():
        pl.semaphore_wait(met.at[2], 2)

    send_modes(0, 0)
    arrived(recv1.at[0, pl.ds(16, 16)], 1)
    x_modes(0, 1)
    send_modes(0, 1)
    send_slab(1, 0, 2)
    send_slab(1, 1, 2)

    @pl.when(jnp.logical_not(far_block))
    def _():
        pl.semaphore_wait(met.at[2], 2)

    arrived(recv2.at[0], 3)
    cot = recv2[0].astype(F32).reshape(256, C)
    row = lax.broadcasted_iota(jnp.int32, (256, C), 0)
    turned = jnp.where(
        lax.rem(row, 2) == 0, pltpu.roll(cot, 255, 0), -pltpu.roll(cot, 1, 0)
    )
    pencil = lax.rem(row // 2, 4)
    back = jnp.zeros((256, C), F32)
    for j in range(4):
        for part, rows in ((0, cot), (1, turned)):
            g = jnp.where(pencil == j, rows, 0.0).astype(BF16)
            big_g[:, pl.ds((2 * j + part) * C, C)] = g
            back += lax.dot_general(
                g, half_v[2 * j + part], (((1,), (1,)), ((), ())), preferred_element_type=F32
            )
    send3[...] = back.astype(BF16).reshape(32, 8, C)
    for b, s in samples[1:]:
        remote(send3.at[b], recv3.at[core, sp], 5, 5 + core, b, s)
    maybe_local(self_in, send3.at[dp], recv3.at[core, sp], 5, 5 + core, *samples[0])

    arrived(recv1.at[1], 2)
    for c in range(2):
        x_modes(1, c)
        send_modes(1, c)

    loads[5].wait()
    for c in range(2):
        arrived(recv3.at[c], 5 + c)
        out4 = dot(bx_v[...], recv3[c].reshape(128, C))
        send4[pl.ds(16 * c, 16)] = out4.astype(BF16).reshape(16, 4, 8, C)
        for s, _ in peers[:-1]:
            remote(send4.at[16 * c + s], modes.at[16 * c + my_block], 7 + c, 7 + c, dp, s)
        local(send4.at[16 * c + sp], modes.at[16 * c + my_block], 7 + c)

    loads[6].wait()
    loads[7].wait()
    arrived(recv2.at[1], 4)
    left = recv2[1].astype(F32).reshape(256, C).T.astype(BF16)
    for n in range(8):
        grads = dot(left, big_g[:, pl.ds(n * C, C)])
        new_w[n], new_first[n], new_second[n] = adam_update(
            w_v[n], first_v[n], second_v[n], grads
        )

    def sent(buf, stage):
        pltpu.make_async_copy(buf, buf, send_sem.at[stage]).wait()

    for c in range(2):
        sent(send1.at[0, pl.ds(0, 15)], c)
        sent(send4.at[pl.ds(0, 15)], 7 + c)
    sent(send1.at[1, pl.ds(0, 30)], 2)

    @pl.when(self_in)
    def _():
        for k in range(2):
            sent(send2.at[k, pl.ds(0, 31)], 3 + k)
        sent(send3.at[pl.ds(0, 31)], 5)

    @pl.when(jnp.logical_not(self_in))
    def _():
        for k in range(2):
            sent(send2.at[k], 3 + k)
        sent(send3, 5)

    for c in range(2):
        arrived(modes.at[pl.ds(16 * c, 16)], 7 + c)


def exchange(field, cot, weights, first, second, yz, fx, bx):
    any_spec = pl.BlockSpec(memory_space=pl.ANY)
    vmem_spec = pl.BlockSpec(memory_space=pltpu.VMEM)
    part = pltpu.VMEM((8, C, C), F32)
    return pl.pallas_call(
        kernel,
        out_shape=(pltpu.VMEM((32, 4, 8, C), BF16), part, part, part),
        in_specs=[any_spec] * 8,
        out_specs=(vmem_spec,) * 4,
        scratch_shapes=[
            pltpu.VMEM((4, 512, C), BF16),
            pltpu.VMEM((4, 512, C), BF16),
            part,
            part,
            part,
            pltpu.VMEM((256, 512), BF16),
            pltpu.VMEM((128, 512), BF16),
            pltpu.VMEM((512, 128), BF16),
            pltpu.VMEM((8, C, C), BF16),
            pltpu.VMEM((2, 32, 4, 8, C), BF16),
            pltpu.VMEM((2, 32, 4, 8, C), BF16),
            pltpu.VMEM((2, 32, 8, C), BF16),
            pltpu.VMEM((2, 32, 8, C), BF16),
            pltpu.VMEM((256, 1024), BF16),
            pltpu.VMEM((32, 8, C), BF16),
            pltpu.VMEM((2, 16, 8, C), BF16),
            pltpu.VMEM((32, 4, 8, C), BF16),
            pltpu.SemaphoreType.DMA((8,)),
            pltpu.SemaphoreType.DMA((9,)),
            pltpu.SemaphoreType.DMA((9,)),
            pltpu.SemaphoreType.REGULAR((3,)),
        ],
        compiler_params=pltpu.CompilerParams(
            collective_id=0, has_side_effects=True, vmem_limit_bytes=VMEM_GRANT
        ),
    )(field, cot, weights, first, second, yz, fx, bx)


def finish_kernel(
    modes, zy, new_w, new_first, new_second, grad_hbm, w_hbm, first_hbm, second_hbm, grad_v, sem
):
    copies = []

    def store(k, src, dst):
        copy = pltpu.make_async_copy(src, dst, sem.at[k])
        copy.start()
        copies.append(copy)

    store(0, new_w, w_hbm)
    store(1, new_first, first_hbm)
    store(2, new_second, second_hbm)
    for x in range(4):
        out = dot(zy[...], modes[:, x].reshape(256, C))
        grad_v[x] = out.astype(BF16)
        store(3 + x, grad_v.at[x], grad_hbm.at[x])
    for copy in copies:
        copy.wait()


def finish(modes, zy, new_w, new_first, new_second):
    any_spec = pl.BlockSpec(memory_space=pl.ANY)
    vmem_spec = pl.BlockSpec(memory_space=pltpu.VMEM)
    part = jax.ShapeDtypeStruct((8, C, C), F32)
    return pl.pallas_call(
        finish_kernel,
        out_shape=(jax.ShapeDtypeStruct((4, 512, C), BF16), part, part, part),
        in_specs=[vmem_spec] * 5,
        out_specs=(any_spec,) * 4,
        scratch_shapes=[pltpu.VMEM((4, 512, C), BF16), pltpu.SemaphoreType.DMA((7,))],
        compiler_params=pltpu.CompilerParams(vmem_limit_bytes=16 * 2**20),
    )(modes, zy, new_w, new_first, new_second)


def adam_update(weights, first_moment, second_moment, weight_grads):
    new_first = decay_first * first_moment + (1.0 - decay_first) * weight_grads
    new_second = decay_second * second_moment + (1.0 - decay_second) * weight_grads * weight_grads
    first_hat = new_first / (1.0 - decay_first**STEP)
    second_hat = new_second / (1.0 - decay_second**STEP)
    new_weights = weights - learn_rate * first_hat / (jnp.sqrt(second_hat) + adam_floor)
    return (new_weights, new_first, new_second)


def on_device(field, cotangent, weights, first_moment, second_moment):
    yz, fx, bx, zy = (jnp.asarray(t) for t in tables())
    modes, new_weights, new_first, new_second = exchange(
        field.reshape(4, 512, C),
        cotangent.reshape(4, 512, C),
        weights.reshape(8, C, C),
        first_moment.reshape(8, C, C),
        second_moment.reshape(8, C, C),
        yz,
        fx,
        bx,
    )
    field_grad, *state = finish(modes, zy, new_weights, new_first, new_second)
    return (field_grad.reshape(field.shape), *(a.reshape(weights.shape) for a in state))


def solution(mesh):
    placed = (
        P("dp", "space", None, None, None),
        P("dp", "space", None, None, None),
        P("space", "dp", None, None, None),
        P("space", "dp", None, None, None),
        P("space", "dp", None, None, None),
    )
    return jax.shard_map(
        on_device,
        mesh=mesh,
        in_specs=placed,
        out_specs=(
            P("dp", "space", None, None, None),
            P("space", "dp", None, None, None),
            P("space", "dp", None, None, None),
            P("space", "dp", None, None, None),
        ),
        check_vma=False,
    )
```

```python
import functools

import jax
import jax.numpy as jnp
import numpy as np
from jax import lax
from jax.experimental import pallas as pl
from jax.experimental.pallas import tpu as pltpu
from jax.sharding import PartitionSpec as P
import ml_dtypes

C = 128
MX = 16
MY = 16
MZ = 8
NX = 64
NY = 32
NZ = 16
STEP = 100
MYZ = 128

decay_first = 0.9
decay_second = 0.999
learn_rate = 0.001
adam_floor = 1e-08

VMEM_GRANT = 64 * 2**20 - 2240 * 1024

MESH = pl.DeviceIdType.MESH
BF16 = jnp.bfloat16
F32 = jnp.float32


def trig_tables(length, modes_kept, signed):
    points = np.arange(length)
    frequency = np.arange(modes_kept) - (modes_kept // 2 if signed else 0)
    phases = np.mod(points[:, None] * frequency[None, :], length).astype(np.float32)
    angles = (phases * np.float32(2.0 * np.pi / length)).astype(np.float32)
    factor = np.float32(1.0 / np.sqrt(length))
    cos_t = (np.cos(angles) * factor).astype(ml_dtypes.bfloat16).astype(np.float32)
    sin_t = (np.sin(angles) * factor).astype(ml_dtypes.bfloat16).astype(np.float32)
    return cos_t, sin_t


def complex_rows(re, im):
    return np.stack([np.stack([re, -im], axis=-1), np.stack([im, re], axis=-1)], axis=1)


@functools.cache
def tables():
    cos_z, sin_z = trig_tables(NZ, MZ, False)
    cos_y, sin_y = trig_tables(NY, MY, True)
    cos_x, sin_x = trig_tables(NX, MX, True)
    ez = cos_z - 1j * sin_z
    ey = cos_y - 1j * sin_y
    ex = cos_x - 1j * sin_x
    yz = np.einsum("ym,zk->mkyz", ey, ez)
    yz = np.stack([yz.real, yz.imag], axis=2).reshape(16, 2, 8, NY * NZ)
    yz = yz.transpose(1, 0, 2, 3).reshape(MYZ * 2, NY * NZ)
    zy = np.einsum("ym,zk->yzmk", ey.conj(), ez.conj())
    zy = np.stack([zy.real, -zy.imag], axis=4).reshape(NY * NZ, 16, 2, 8)
    zy = zy.transpose(0, 2, 1, 3).reshape(NY * NZ, MYZ * 2)
    eye = np.eye(4)
    fx = complex_rows(ex.T.real, ex.T.imag)
    fx = np.einsum("msxr,pq->mpsxqr", fx, eye).reshape(MX * 8, NX * 8)
    bx = complex_rows(ex.conj().real, ex.conj().imag)
    bx = np.einsum("xsmr,pq->xpsmqr", bx, eye).reshape(NX * 8, MX * 8)
    return tuple(t.astype(ml_dtypes.bfloat16) for t in (yz, fx, bx, zy))


def tri(v):
    return ((v * (v + 1)) >> 1) & 3


def dot(a, b):
    return jnp.dot(a, b, preferred_element_type=F32)


def kernel(
    field_hbm,
    cot_hbm,
    w_hbm,
    first_hbm,
    second_hbm,
    yz_hbm,
    fx_hbm,
    bx_hbm,
    modes,
    new_w,
    new_first,
    new_second,
    cot_v,
    field_v,
    w_v,
    first_v,
    second_v,
    yz_v,
    fx_v,
    bx_v,
    half_v,
    send1,
    recv1,
    send2,
    recv2,
    big_g,
    send3,
    recv3,
    send4,
    in_sem,
    send_sem,
    recv_sem,
    met,
):
    dp = lax.axis_index("dp")
    sp = lax.axis_index("space")

    def load(k, src, dst):
        copy = pltpu.make_async_copy(src, dst, in_sem.at[k])
        copy.start()
        return copy

    loads = [load(0, yz_hbm, yz_v), load(1, cot_hbm, cot_v)]

    def hello(sem, b, s):
        pl.semaphore_signal(sem, inc=1, device_id=(b, s), device_id_type=MESH)

    barrier = pltpu.get_barrier_semaphore()
    core = dp & 1
    first_core = core == 0
    second_core = core == 1
    chip = dp - core
    for k in range(16):

        @pl.when(jnp.logical_or(sp != k, second_core))
        def _():
            hello(barrier, chip, k)

    gx, gz = dp >> 3, (dp >> 1) & 3
    sy, sz = sp >> 2, sp & 3
    mine = dp >> 1
    mx, mz = mine >> 2, mine & 3

    half_way = (sz + 2) & 3
    peer_z = (3 - sz, half_way, 3 - half_way, sz)
    peer_y = tuple((sy + i) & 3 for i in range(4))
    block_y = tuple(((gx + y + 2 * core) & 3) * 4 for y in peer_y)
    block_z = tuple((gz + 3 + (1 + 2 * core) * tri(z)) & 3 for z in peer_z)
    peers = [
        (peer_y[iy] * 4 + peer_z[iz], block_y[iy] + block_z[iz])
        for iz in range(4)
        for iy in (2, 1, 3, 0)
    ]
    my_block = peers[-1][1]
    self_in = my_block == mine

    at_y, at_z, sample = {}, {}, {}
    for ic in range(2):
        c = (core + ic) & 1
        for i in range(4):
            x, z = (gx + i) & 3, (gz + i) & 3
            at_y[i, ic] = ((mx - x - 2 * c + 8) & 3) * 4
            at_z[i, ic] = tri(((1 + 2 * c) * (mz - z + 5)) & 3)
            sample["x", i] = x * 8
            sample["z", i] = z * 2
        sample["c", ic] = c
    samples = []
    for iz in (0, 2, 1, 3):
        for ix in (0, 2, 1, 3):
            for ic in range(2):
                b = sample["x", ix] + sample["z", iz] + sample["c", ic]
                samples.append((b, at_y[ix, ic] + at_z[iz, ic]))

    for b, s in samples[2:]:
        hello(barrier, b | 1, s)
    for b, s in samples[:2]:

        @pl.when(jnp.logical_or(first_core, s != sp))
        def _():
            hello(barrier, b | 1, s)

    own_holder = jnp.logical_or(samples[0][1] == sp, samples[1][1] == sp)

    def remote(src, dst, send, recv, b, s):
        pltpu.make_async_remote_copy(
            src_ref=src,
            dst_ref=dst,
            send_sem=send_sem.at[send],
            recv_sem=recv_sem.at[recv],
            device_id=(b, s),
            device_id_type=MESH,
        ).start()

    def local(src, dst, recv):
        pltpu.make_async_copy(src, dst, recv_sem.at[recv]).start()

    def maybe_local(here, src, dst, send, recv, b, s):
        @pl.when(here)
        def _():
            local(src, dst, recv)

        @pl.when(jnp.logical_not(here))
        def _():
            remote(src, dst, send, recv, b, s)

    def arrived(buf, stage):
        with jax.named_scope(f"wait_recv{stage}"):
            pltpu.make_async_copy(buf, buf, recv_sem.at[stage]).wait()

    def yz_modes(k, slab):
        for x in range(4):
            out = dot(yz_v[...], slab[x])
            send1[k, :, x] = out.astype(BF16).reshape(32, 8, C)

    def send_slab(k, c, stage):
        for s, q in peers[:-1]:
            remote(send1.at[k, 16 * c + q], recv1.at[k, 16 * c + sp], stage, stage, dp, s)
        local(send1.at[k, 16 * c + my_block], recv1.at[k, 16 * c + sp], stage)

    def x_modes(k, c):
        slab = recv1[k, pl.ds(16 * c, 16)].reshape(512, C)
        send2[k, pl.ds(16 * c, 16)] = dot(fx_v[...], slab).astype(BF16).reshape(16, 8, C)

    def send_modes(k, c):
        b = 2 * my_block + c
        for i in range(1, 16):
            s = (sp + i) & 15
            remote(send2.at[k, 16 * c + s], recv2.at[k, dp], 3 + k, 3 + k, b, s)
        here = jnp.logical_and(self_in, core == c)
        maybe_local(here, send2.at[k, 16 * c + sp], recv2.at[k, dp], 3 + k, 3 + k, b, sp)

    loads[0].wait()
    loads[1].wait()
    loads += [
        load(2, field_hbm, field_v),
        load(3, fx_hbm, fx_v),
        load(4, w_hbm, w_v),
        load(5, bx_hbm, bx_v),
        load(6, first_hbm, first_v),
        load(7, second_hbm, second_v),
    ]
    yz_modes(0, cot_v)

    with jax.named_scope("wait_barrier"):

        @pl.when(first_core)
        def _():
            pl.semaphore_wait(barrier, 31)
            hello(met.at[0], dp + 1, sp)

        @pl.when(second_core)
        def _():
            pl.semaphore_wait(met.at[0], 1)

    send_slab(0, 0, 0)
    send_slab(0, 1, 1)
    loads[2].wait()
    yz_modes(1, field_v)
    loads[3].wait()
    loads[4].wait()
    half_v[...] = w_v[...].astype(BF16)

    @pl.when(second_core)
    def _():
        @pl.when(own_holder)
        def _():
            pl.semaphore_wait(barrier, 63)

        @pl.when(jnp.logical_not(own_holder))
        def _():
            pl.semaphore_wait(barrier, 64)

        hello(met.at[1], chip, sp)

    arrived(recv1.at[0, pl.ds(0, 16)], 0)
    x_modes(0, 0)

    @pl.when(first_core)
    def _():
        with jax.named_scope("wait_far0"):
            pl.semaphore_wait(met.at[1], 1)

    send_modes(0, 0)
    arrived(recv1.at[0, pl.ds(16, 16)], 1)
    x_modes(0, 1)
    send_modes(0, 1)
    send_slab(1, 0, 2)
    send_slab(1, 1, 2)

    arrived(recv2.at[0], 3)
    cot = recv2[0].astype(F32).reshape(256, C)
    row = lax.broadcasted_iota(jnp.int32, (256, C), 0)
    turned = jnp.where(
        lax.rem(row, 2) == 0, pltpu.roll(cot, 255, 0), -pltpu.roll(cot, 1, 0)
    )
    pencil = lax.rem(row // 2, 4)
    back = jnp.zeros((256, C), F32)
    for j in range(4):
        for part, rows in ((0, cot), (1, turned)):
            g = jnp.where(pencil == j, rows, 0.0).astype(BF16)
            big_g[:, pl.ds((2 * j + part) * C, C)] = g
            back += lax.dot_general(
                g, half_v[2 * j + part], (((1,), (1,)), ((), ())), preferred_element_type=F32
            )
    send3[...] = back.astype(BF16).reshape(32, 8, C)
    for b, s in samples[1:]:
        remote(send3.at[b], recv3.at[core, sp], 5, 5 + core, b, s)
    maybe_local(self_in, send3.at[dp], recv3.at[core, sp], 5, 5 + core, *samples[0])

    arrived(recv1.at[1], 2)
    for c in range(2):
        x_modes(1, c)
        send_modes(1, c)

    loads[5].wait()
    for c in range(2):
        arrived(recv3.at[c], 5 + c)
        out4 = dot(bx_v[...], recv3[c].reshape(128, C))
        send4[pl.ds(16 * c, 16)] = out4.astype(BF16).reshape(16, 4, 8, C)
        for s, _ in peers[:-1]:
            remote(send4.at[16 * c + s], modes.at[16 * c + my_block], 7 + c, 7 + c, dp, s)
        local(send4.at[16 * c + sp], modes.at[16 * c + my_block], 7 + c)

    loads[6].wait()
    loads[7].wait()
    arrived(recv2.at[1], 4)
    left = recv2[1].astype(F32).reshape(256, C).T.astype(BF16)
    for n in range(8):
        grads = dot(left, big_g[:, pl.ds(n * C, C)])
        new_w[n], new_first[n], new_second[n] = adam_update(
            w_v[n], first_v[n], second_v[n], grads
        )

    def sent(buf, stage):
        pltpu.make_async_copy(buf, buf, send_sem.at[stage]).wait()

    for c in range(2):
        sent(send1.at[0, pl.ds(0, 15)], c)
        sent(send4.at[pl.ds(0, 15)], 7 + c)
    sent(send1.at[1, pl.ds(0, 30)], 2)

    @pl.when(self_in)
    def _():
        for k in range(2):
            sent(send2.at[k, pl.ds(0, 31)], 3 + k)
        sent(send3.at[pl.ds(0, 31)], 5)

    @pl.when(jnp.logical_not(self_in))
    def _():
        for k in range(2):
            sent(send2.at[k], 3 + k)
        sent(send3, 5)

    for c in range(2):
        arrived(modes.at[pl.ds(16 * c, 16)], 7 + c)


def exchange(field, cot, weights, first, second, yz, fx, bx):
    any_spec = pl.BlockSpec(memory_space=pl.ANY)
    vmem_spec = pl.BlockSpec(memory_space=pltpu.VMEM)
    part = pltpu.VMEM((8, C, C), F32)
    return pl.pallas_call(
        kernel,
        out_shape=(pltpu.VMEM((32, 4, 8, C), BF16), part, part, part),
        in_specs=[any_spec] * 8,
        out_specs=(vmem_spec,) * 4,
        scratch_shapes=[
            pltpu.VMEM((4, 512, C), BF16),
            pltpu.VMEM((4, 512, C), BF16),
            part,
            part,
            part,
            pltpu.VMEM((256, 512), BF16),
            pltpu.VMEM((128, 512), BF16),
            pltpu.VMEM((512, 128), BF16),
            pltpu.VMEM((8, C, C), BF16),
            pltpu.VMEM((2, 32, 4, 8, C), BF16),
            pltpu.VMEM((2, 32, 4, 8, C), BF16),
            pltpu.VMEM((2, 32, 8, C), BF16),
            pltpu.VMEM((2, 32, 8, C), BF16),
            pltpu.VMEM((256, 1024), BF16),
            pltpu.VMEM((32, 8, C), BF16),
            pltpu.VMEM((2, 16, 8, C), BF16),
            pltpu.VMEM((32, 4, 8, C), BF16),
            pltpu.SemaphoreType.DMA((8,)),
            pltpu.SemaphoreType.DMA((9,)),
            pltpu.SemaphoreType.DMA((9,)),
            pltpu.SemaphoreType.REGULAR((2,)),
        ],
        compiler_params=pltpu.CompilerParams(
            collective_id=0, has_side_effects=True, vmem_limit_bytes=VMEM_GRANT
        ),
    )(field, cot, weights, first, second, yz, fx, bx)


def finish_kernel(
    modes, zy, new_w, new_first, new_second, grad_hbm, w_hbm, first_hbm, second_hbm, grad_v, sem
):
    copies = []

    def store(k, src, dst):
        copy = pltpu.make_async_copy(src, dst, sem.at[k])
        copy.start()
        copies.append(copy)

    store(0, new_w, w_hbm)
    store(1, new_first, first_hbm)
    store(2, new_second, second_hbm)
    for x in range(4):
        out = dot(zy[...], modes[:, x].reshape(256, C))
        grad_v[x] = out.astype(BF16)
        store(3 + x, grad_v.at[x], grad_hbm.at[x])
    for copy in copies:
        copy.wait()


def finish(modes, zy, new_w, new_first, new_second):
    any_spec = pl.BlockSpec(memory_space=pl.ANY)
    vmem_spec = pl.BlockSpec(memory_space=pltpu.VMEM)
    part = jax.ShapeDtypeStruct((8, C, C), F32)
    return pl.pallas_call(
        finish_kernel,
        out_shape=(jax.ShapeDtypeStruct((4, 512, C), BF16), part, part, part),
        in_specs=[vmem_spec] * 5,
        out_specs=(any_spec,) * 4,
        scratch_shapes=[pltpu.VMEM((4, 512, C), BF16), pltpu.SemaphoreType.DMA((7,))],
        compiler_params=pltpu.CompilerParams(vmem_limit_bytes=16 * 2**20),
    )(modes, zy, new_w, new_first, new_second)


def adam_update(weights, first_moment, second_moment, weight_grads):
    new_first = decay_first * first_moment + (1.0 - decay_first) * weight_grads
    new_second = decay_second * second_moment + (1.0 - decay_second) * weight_grads * weight_grads
    first_hat = new_first / (1.0 - decay_first**STEP)
    second_hat = new_second / (1.0 - decay_second**STEP)
    new_weights = weights - learn_rate * first_hat / (jnp.sqrt(second_hat) + adam_floor)
    return (new_weights, new_first, new_second)


def on_device(field, cotangent, weights, first_moment, second_moment):
    yz, fx, bx, zy = (jnp.asarray(t) for t in tables())
    modes, new_weights, new_first, new_second = exchange(
        field.reshape(4, 512, C),
        cotangent.reshape(4, 512, C),
        weights.reshape(8, C, C),
        first_moment.reshape(8, C, C),
        second_moment.reshape(8, C, C),
        yz,
        fx,
        bx,
    )
    field_grad, *state = finish(modes, zy, new_weights, new_first, new_second)
    return (field_grad.reshape(field.shape), *(a.reshape(weights.shape) for a in state))


def solution(mesh):
    placed = (
        P("dp", "space", None, None, None),
        P("dp", "space", None, None, None),
        P("space", "dp", None, None, None),
        P("space", "dp", None, None, None),
        P("space", "dp", None, None, None),
    )
    return jax.shard_map(
        on_device,
        mesh=mesh,
        in_specs=placed,
        out_specs=(
            P("dp", "space", None, None, None),
            P("space", "dp", None, None, None),
            P("space", "dp", None, None, None),
            P("space", "dp", None, None, None),
        ),
        check_vma=False,
    )
```

```python
import functools

import jax
import jax.numpy as jnp
import numpy as np
from jax import lax
from jax.experimental import pallas as pl
from jax.experimental.pallas import tpu as pltpu
from jax.sharding import PartitionSpec as P
import ml_dtypes

C = 128
MX = 16
MY = 16
MZ = 8
NX = 64
NY = 32
NZ = 16
STEP = 100
MYZ = 128

decay_first = 0.9
decay_second = 0.999
learn_rate = 0.001
adam_floor = 1e-08

VMEM_GRANT = 64 * 2**20 - 2240 * 1024

MESH = pl.DeviceIdType.MESH
BF16 = jnp.bfloat16
F32 = jnp.float32


def trig_tables(length, modes_kept, signed):
    points = np.arange(length)
    frequency = np.arange(modes_kept) - (modes_kept // 2 if signed else 0)
    phases = np.mod(points[:, None] * frequency[None, :], length).astype(np.float32)
    angles = (phases * np.float32(2.0 * np.pi / length)).astype(np.float32)
    factor = np.float32(1.0 / np.sqrt(length))
    cos_t = (np.cos(angles) * factor).astype(ml_dtypes.bfloat16).astype(np.float32)
    sin_t = (np.sin(angles) * factor).astype(ml_dtypes.bfloat16).astype(np.float32)
    return cos_t, sin_t


def complex_rows(re, im):
    return np.stack([np.stack([re, -im], axis=-1), np.stack([im, re], axis=-1)], axis=1)


@functools.cache
def tables():
    cos_z, sin_z = trig_tables(NZ, MZ, False)
    cos_y, sin_y = trig_tables(NY, MY, True)
    cos_x, sin_x = trig_tables(NX, MX, True)
    ez = cos_z - 1j * sin_z
    ey = cos_y - 1j * sin_y
    ex = cos_x - 1j * sin_x
    yz = np.einsum("ym,zk->mkyz", ey, ez)
    yz = np.stack([yz.real, yz.imag], axis=2).reshape(16, 2, 8, NY * NZ)
    yz = yz.transpose(1, 0, 2, 3).reshape(MYZ * 2, NY * NZ)
    zy = np.einsum("ym,zk->yzmk", ey.conj(), ez.conj())
    zy = np.stack([zy.real, -zy.imag], axis=4).reshape(NY * NZ, 16, 2, 8)
    zy = zy.transpose(0, 2, 1, 3).reshape(NY * NZ, MYZ * 2)
    eye = np.eye(4)
    fx = complex_rows(ex.T.real, ex.T.imag)
    fx = np.einsum("msxr,pq->mpsxqr", fx, eye).reshape(MX * 8, NX * 8)
    bx = complex_rows(ex.conj().real, ex.conj().imag)
    bx = np.einsum("xsmr,pq->xpsmqr", bx, eye).reshape(NX * 8, MX * 8)
    return tuple(t.astype(ml_dtypes.bfloat16) for t in (yz, fx, bx, zy))


def tri(v):
    return ((v * (v + 1)) >> 1) & 3


def dot(a, b):
    return jnp.dot(a, b, preferred_element_type=F32)


def kernel(
    field_hbm,
    cot_hbm,
    w_hbm,
    first_hbm,
    second_hbm,
    yz_hbm,
    fx_hbm,
    bx_hbm,
    zy_hbm,
    grad,
    new_w,
    new_first,
    new_second,
    cot_v,
    field_v,
    w_v,
    first_v,
    second_v,
    yz_v,
    fx_v,
    bx_v,
    zy_v,
    half_v,
    send1,
    recv1,
    send2,
    recv2,
    big_g,
    send3,
    recv3,
    send4,
    modes,
    part_v,
    in_sem,
    send_sem,
    recv_sem,
    met,
):
    dp = lax.axis_index("dp")
    sp = lax.axis_index("space")

    def load(k, src, dst):
        copy = pltpu.make_async_copy(src, dst, in_sem.at[k])
        copy.start()
        return copy

    loads = [load(0, yz_hbm, yz_v), load(1, cot_hbm, cot_v)]

    def hello(sem, b, s):
        pl.semaphore_signal(sem, inc=1, device_id=(b, s), device_id_type=MESH)

    barrier = pltpu.get_barrier_semaphore()
    core = dp & 1
    first_core = core == 0
    second_core = core == 1
    chip = dp - core
    gx, gz = dp >> 3, (dp >> 1) & 3
    sy, sz = sp >> 2, sp & 3

    mine = dp >> 1
    mx, mz = mine >> 2, mine & 3
    at_y, at_z = {}, {}
    for ic in range(2):
        c = (core + ic) & 1
        for i in range(4):
            x = (gx + i) & 3
            at_y[i, ic] = (x * 8 + c, x * 2 + c, ((mx - x - 2 * c + 8) & 3) * 4)
            at_z[i, ic] = tri(((1 + 2 * c) * (mz - i + 5)) & 3)
    samples = [
        [
            (at_y[i, ic][0] + 2 * z, at_y[i, ic][1] + 8 * (0, 1, 3, 2)[z], at_y[i, ic][2] + at_z[z, ic])
            for i in (0, 2, 1, 3)
            for ic in range(2)
        ]
        for z in range(4)
    ]

    def hello_holders(z):
        for b, _, s in samples[z][2:]:
            hello(barrier, b | 1, s)
        for b, _, s in samples[z][:2]:

            @pl.when(jnp.logical_or(first_core, jnp.logical_or(gz != z, s != sp)))
            def _():
                hello(barrier, b | 1, s)

    hello_holders(0)
    for k in range(16):

        @pl.when(jnp.logical_or(sp != k, second_core))
        def _():
            hello(barrier, chip, k)

    for z in range(1, 4):
        hello_holders(z)

    own_holder = sp < 0
    for z in range(4):
        for _, _, s in samples[z][:2]:
            own_holder = jnp.logical_or(own_holder, jnp.logical_and(gz == z, s == sp))


    half_way = (sz + 2) & 3
    peer_z = (3 - sz, half_way, 3 - half_way, sz)
    peer_y = tuple((sy + i) & 3 for i in range(4))
    block_y = tuple(((gx + y + 2 * core) & 3) * 4 for y in peer_y)
    block_z = tuple((gz + 3 + (1 + 2 * core) * tri(z)) & 3 for z in peer_z)
    peers = [
        (peer_y[iy] * 4 + peer_z[iz], block_y[iy] + block_z[iz])
        for iz in range(4)
        for iy in (2, 1, 3, 0)
    ]
    my_block = peers[-1][1]
    self_in = my_block == mine
    rank = tri(gz)
    my_slot = rank * 8 + gx * 2 + core
    batch = (3 + 6 * jnp.minimum(rank, 1) + ((rank + 1) >> 2), 4)

    def remote(src, dst, send, recv, b, s):
        pltpu.make_async_remote_copy(
            src_ref=src,
            dst_ref=dst,
            send_sem=send_sem.at[send],
            recv_sem=recv_sem.at[recv],
            device_id=(b, s),
            device_id_type=MESH,
        ).start()

    def local(src, dst, recv):
        pltpu.make_async_copy(src, dst, recv_sem.at[recv]).start()

    def maybe_local(here, src, dst, send, recv, b, s):
        @pl.when(here)
        def _():
            local(src, dst, recv)

        @pl.when(jnp.logical_not(here))
        def _():
            remote(src, dst, send, recv, b, s)

    def arrived(buf, stage):
        with jax.named_scope(f"wait_recv{stage}"):
            pltpu.make_async_copy(buf, buf, recv_sem.at[stage]).wait()

    def yz_modes(k, slab):
        for x in range(4):
            out = dot(yz_v[...], slab[x])
            send1[k, :, x] = out.astype(BF16).reshape(32, 8, C)

    def send_slab(k, c, stage):
        for s, q in peers[:-1]:
            remote(send1.at[k, 16 * c + q], recv1.at[k, 16 * c + sp], stage, stage, dp, s)
        local(send1.at[k, 16 * c + my_block], recv1.at[k, 16 * c + sp], stage)

    def x_modes(k, c):
        slab = recv1[k, pl.ds(16 * c, 16)].reshape(512, C)
        send2[k, pl.ds(16 * c, 16)] = dot(fx_v[...], slab).astype(BF16).reshape(16, 8, C)

    def send_modes(k, c):
        b = 2 * my_block + c
        for i in range(1, 16):
            s = (sp + i) & 15
            remote(send2.at[k, 16 * c + s], recv2.at[k, my_slot], 3 + k, batch[k], b, s)
        here = jnp.logical_and(self_in, core == c)
        maybe_local(
            here, send2.at[k, 16 * c + sp], recv2.at[k, my_slot], 3 + k, batch[k], b, sp
        )

    loads[0].wait()
    loads[1].wait()
    loads += [
        load(2, field_hbm, field_v),
        load(3, fx_hbm, fx_v),
        load(4, w_hbm, w_v),
        load(5, bx_hbm, bx_v),
        load(6, first_hbm, first_v),
        load(7, second_hbm, second_v),
        load(8, zy_hbm, zy_v),
    ]
    yz_modes(0, cot_v)

    with jax.named_scope("wait_barrier"):

        @pl.when(first_core)
        def _():
            pl.semaphore_wait(barrier, 31)
            hello(met.at[0], dp + 1, sp)

        @pl.when(second_core)
        def _():
            pl.semaphore_wait(met.at[0], 1)

    send_slab(0, 0, 0)
    send_slab(0, 1, 1)
    loads[2].wait()
    yz_modes(1, field_v)
    loads[3].wait()
    loads[4].wait()
    half_v[...] = w_v[...].astype(BF16)

    @pl.when(second_core)
    def _():
        @pl.when(own_holder)
        def _():
            pl.semaphore_wait(barrier, 63)

        @pl.when(jnp.logical_not(own_holder))
        def _():
            pl.semaphore_wait(barrier, 64)

        hello(met.at[1], chip, sp)

    arrived(recv1.at[0, pl.ds(0, 16)], 0)
    x_modes(0, 0)

    @pl.when(first_core)
    def _():
        with jax.named_scope("wait_far0"):
            pl.semaphore_wait(met.at[1], 1)

    send_modes(0, 0)
    arrived(recv1.at[0, pl.ds(16, 16)], 1)
    x_modes(0, 1)
    send_modes(0, 1)
    send_slab(1, 0, 2)
    send_slab(1, 1, 2)

    def mode_grads(first, count):
        cot = recv2[0, pl.ds(first, count)].astype(F32).reshape(8 * count, C)
        row = lax.broadcasted_iota(jnp.int32, cot.shape, 0)
        turned = jnp.where(
            lax.rem(row, 2) == 0, pltpu.roll(cot, 8 * count - 1, 0), -pltpu.roll(cot, 1, 0)
        )
        pencil = lax.rem(row // 2, 4)
        back = jnp.zeros(cot.shape, F32)
        for j in range(4):
            for part, rows in ((0, cot), (1, turned)):
                g = jnp.where(pencil == j, rows, 0.0).astype(BF16)
                big_g[pl.ds(8 * first, 8 * count), pl.ds((2 * j + part) * C, C)] = g
                back += lax.dot_general(
                    g, half_v[2 * j + part], (((1,), (1,)), ((), ())), preferred_element_type=F32
                )
        send3[pl.ds(first, count)] = back.astype(BF16).reshape(count, 8, C)

    def send_grads(z):
        for b, slot, s in samples[z][1:]:
            remote(send3.at[slot], recv3.at[core, sp], 5, 5 + core, b, s)
        b, slot, s = samples[z][0]
        here = jnp.logical_and(self_in, gz == z)
        maybe_local(here, send3.at[slot], recv3.at[core, sp], 5, 5 + core, b, s)

    arrived(recv2.at[0, pl.ds(0, 8)], 3)
    mode_grads(0, 8)
    send_grads(0)
    arrived(recv2.at[0, pl.ds(8, 16)], 9)
    mode_grads(8, 16)
    send_grads(1)
    send_grads(3)
    arrived(recv1.at[1], 2)
    for c in range(2):
        x_modes(1, c)
        send_modes(1, c)
    arrived(recv2.at[0, pl.ds(24, 8)], 10)
    mode_grads(24, 8)
    send_grads(2)

    loads[5].wait()
    for c in range(2):
        arrived(recv3.at[c], 5 + c)
        out4 = dot(bx_v[...], recv3[c].reshape(128, C))
        send4[pl.ds(16 * c, 16)] = out4.astype(BF16).reshape(16, 4, 8, C)
        for s, _ in peers[:-1]:
            remote(send4.at[16 * c + s], modes.at[16 * c + my_block], 7 + c, 7 + c, dp, s)
        local(send4.at[16 * c + sp], modes.at[16 * c + my_block], 7 + c)

    loads[6].wait()
    loads[7].wait()
    arrived(recv2.at[1], 4)
    left = recv2[1].astype(F32).reshape(256, C).T.astype(BF16)
    for n in range(8):
        grads = dot(left, big_g[:, pl.ds(n * C, C)])
        new_w[n], new_first[n], new_second[n] = adam_update(
            w_v[n], first_v[n], second_v[n], grads
        )

    def sent(buf, stage):
        pltpu.make_async_copy(buf, buf, send_sem.at[stage]).wait()

    for c in range(2):
        sent(send1.at[0, pl.ds(0, 15)], c)
        sent(send4.at[pl.ds(0, 15)], 7 + c)
    sent(send1.at[1, pl.ds(0, 30)], 2)

    @pl.when(self_in)
    def _():
        for k in range(2):
            sent(send2.at[k, pl.ds(0, 31)], 3 + k)
        sent(send3.at[pl.ds(0, 31)], 5)

    @pl.when(jnp.logical_not(self_in))
    def _():
        for k in range(2):
            sent(send2.at[k], 3 + k)
        sent(send3, 5)

    loads[8].wait()
    for c in range(2):
        arrived(modes.at[pl.ds(16 * c, 16)], 7 + c)
        for x in range(4):
            half = modes[pl.ds(16 * c, 16), x].reshape(128, C)
            term = dot(zy_v[:, pl.ds(128 * c, 128)], half)
            if c == 0:
                part_v[x] = term
            else:
                grad[x] = (part_v[x] + term).astype(BF16)


def exchange(field, cot, weights, first, second, yz, fx, bx, zy):
    any_spec = pl.BlockSpec(memory_space=pl.ANY)
    vmem_spec = pl.BlockSpec(memory_space=pltpu.VMEM)
    part = pltpu.VMEM((8, C, C), F32)
    return pl.pallas_call(
        kernel,
        out_shape=(pltpu.VMEM((4, 512, C), BF16), part, part, part),
        in_specs=[any_spec] * 9,
        out_specs=(vmem_spec,) * 4,
        scratch_shapes=[
            pltpu.VMEM((4, 512, C), BF16),
            pltpu.VMEM((4, 512, C), BF16),
            part,
            part,
            part,
            pltpu.VMEM((256, 512), BF16),
            pltpu.VMEM((128, 512), BF16),
            pltpu.VMEM((512, 128), BF16),
            pltpu.VMEM((512, 256), BF16),
            pltpu.VMEM((8, C, C), BF16),
            pltpu.VMEM((2, 32, 4, 8, C), BF16),
            pltpu.VMEM((2, 32, 4, 8, C), BF16),
            pltpu.VMEM((2, 32, 8, C), BF16),
            pltpu.VMEM((2, 32, 8, C), BF16),
            pltpu.VMEM((256, 1024), BF16),
            pltpu.VMEM((32, 8, C), BF16),
            pltpu.VMEM((2, 16, 8, C), BF16),
            pltpu.VMEM((32, 4, 8, C), BF16),
            pltpu.VMEM((32, 4, 8, C), BF16),
            pltpu.VMEM((4, 512, C), F32),
            pltpu.SemaphoreType.DMA((9,)),
            pltpu.SemaphoreType.DMA((9,)),
            pltpu.SemaphoreType.DMA((11,)),
            pltpu.SemaphoreType.REGULAR((2,)),
        ],
        compiler_params=pltpu.CompilerParams(
            collective_id=0, has_side_effects=True, vmem_limit_bytes=VMEM_GRANT
        ),
    )(field, cot, weights, first, second, yz, fx, bx, zy)


def finish_kernel(*refs):
    sources, targets, sem = refs[:4], refs[4:8], refs[8]
    copies = []
    for src, dst in zip(sources, targets, strict=True):
        rows = src.shape[0] // 4
        for i in range(4):
            span = pl.ds(i * rows, rows)
            copies.append(pltpu.make_async_copy(src.at[span], dst.at[span], sem.at[len(copies)]))
            copies[-1].start()
    for copy in copies:
        copy.wait()


def finish(*results):
    return pl.pallas_call(
        finish_kernel,
        out_shape=tuple(jax.ShapeDtypeStruct(r.shape, r.dtype) for r in results),
        in_specs=[pl.BlockSpec(memory_space=pltpu.VMEM)] * 4,
        out_specs=(pl.BlockSpec(memory_space=pl.ANY),) * 4,
        scratch_shapes=[pltpu.SemaphoreType.DMA((16,))],
        compiler_params=pltpu.CompilerParams(vmem_limit_bytes=16 * 2**20),
    )(*results)


def adam_update(weights, first_moment, second_moment, weight_grads):
    new_first = decay_first * first_moment + (1.0 - decay_first) * weight_grads
    new_second = decay_second * second_moment + (1.0 - decay_second) * weight_grads * weight_grads
    first_hat = new_first / (1.0 - decay_first**STEP)
    second_hat = new_second / (1.0 - decay_second**STEP)
    new_weights = weights - learn_rate * first_hat / (jnp.sqrt(second_hat) + adam_floor)
    return (new_weights, new_first, new_second)


def on_device(field, cotangent, weights, first_moment, second_moment):
    yz, fx, bx, zy = (jnp.asarray(t) for t in tables())
    results = exchange(
        field.reshape(4, 512, C),
        cotangent.reshape(4, 512, C),
        weights.reshape(8, C, C),
        first_moment.reshape(8, C, C),
        second_moment.reshape(8, C, C),
        yz,
        fx,
        bx,
        zy,
    )
    field_grad, *state = finish(*results)
    return (field_grad.reshape(field.shape), *(a.reshape(weights.shape) for a in state))


def solution(mesh):
    placed = (
        P("dp", "space", None, None, None),
        P("dp", "space", None, None, None),
        P("space", "dp", None, None, None),
        P("space", "dp", None, None, None),
        P("space", "dp", None, None, None),
    )
    return jax.shard_map(
        on_device,
        mesh=mesh,
        in_specs=placed,
        out_specs=(
            P("dp", "space", None, None, None),
            P("space", "dp", None, None, None),
            P("space", "dp", None, None, None),
            P("space", "dp", None, None, None),
        ),
        check_vma=False,
    )
```

```python
import functools

import jax
import jax.numpy as jnp
import numpy as np
from jax import lax
from jax.experimental import pallas as pl
from jax.experimental.pallas import tpu as pltpu
from jax.sharding import PartitionSpec as P
import ml_dtypes

C = 128
MX = 16
MY = 16
MZ = 8
NX = 64
NY = 32
NZ = 16
STEP = 100
MYZ = 128

decay_first = 0.9
decay_second = 0.999
learn_rate = 0.001
adam_floor = 1e-08

VMEM_GRANT = 64 * 2**20 - 2240 * 1024

MESH = pl.DeviceIdType.MESH
BF16 = jnp.bfloat16
F32 = jnp.float32


def trig_tables(length, modes_kept, signed):
    points = np.arange(length)
    frequency = np.arange(modes_kept) - (modes_kept // 2 if signed else 0)
    phases = np.mod(points[:, None] * frequency[None, :], length).astype(np.float32)
    angles = (phases * np.float32(2.0 * np.pi / length)).astype(np.float32)
    factor = np.float32(1.0 / np.sqrt(length))
    cos_t = (np.cos(angles) * factor).astype(ml_dtypes.bfloat16).astype(np.float32)
    sin_t = (np.sin(angles) * factor).astype(ml_dtypes.bfloat16).astype(np.float32)
    return cos_t, sin_t


def complex_rows(re, im):
    return np.stack([np.stack([re, -im], axis=-1), np.stack([im, re], axis=-1)], axis=1)


@functools.cache
def tables():
    cos_z, sin_z = trig_tables(NZ, MZ, False)
    cos_y, sin_y = trig_tables(NY, MY, True)
    cos_x, sin_x = trig_tables(NX, MX, True)
    ez = cos_z - 1j * sin_z
    ey = cos_y - 1j * sin_y
    ex = cos_x - 1j * sin_x
    yz = np.einsum("ym,zk->mkyz", ey, ez)
    yz = np.stack([yz.real, yz.imag], axis=2).reshape(16, 2, 8, NY * NZ)
    yz = yz.transpose(1, 0, 2, 3).reshape(MYZ * 2, NY * NZ)
    zy = np.einsum("ym,zk->yzmk", ey.conj(), ez.conj())
    zy = np.stack([zy.real, -zy.imag], axis=4).reshape(NY * NZ, 16, 2, 8)
    zy = zy.transpose(0, 2, 1, 3).reshape(NY * NZ, MYZ * 2)
    eye = np.eye(4)
    fx = complex_rows(ex.T.real, ex.T.imag)
    fx = np.einsum("msxr,pq->mpsxqr", fx, eye).reshape(MX * 8, NX * 8)
    bx = complex_rows(ex.conj().real, ex.conj().imag)
    bx = np.einsum("xsmr,pq->xpsmqr", bx, eye).reshape(NX * 8, MX * 8)
    return tuple(t.astype(ml_dtypes.bfloat16) for t in (yz, fx, bx, zy))


def tri(v):
    return ((v * (v + 1)) >> 1) & 3


def dot(a, b):
    return jnp.dot(a, b, preferred_element_type=F32)


def kernel(
    field_hbm,
    cot_hbm,
    w_hbm,
    first_hbm,
    second_hbm,
    yz_hbm,
    fx_hbm,
    bx_hbm,
    zy_hbm,
    grad,
    new_w,
    new_first,
    new_second,
    cot_v,
    field_v,
    w_v,
    first_v,
    second_v,
    yz_v,
    fx_v,
    bx_v,
    zy_v,
    half_v,
    send1,
    recv1,
    send2,
    recv2,
    big_g,
    send3,
    recv3,
    send4,
    modes,
    part_v,
    in_sem,
    send_sem,
    recv_sem,
    met,
):
    dp = lax.axis_index("dp")
    sp = lax.axis_index("space")

    def load(k, src, dst):
        copy = pltpu.make_async_copy(src, dst, in_sem.at[k])
        copy.start()
        return copy

    loads = [load(0, yz_hbm, yz_v), load(1, cot_hbm, cot_v)]

    def hello(sem, b, s):
        pl.semaphore_signal(sem, inc=1, device_id=(b, s), device_id_type=MESH)

    barrier = pltpu.get_barrier_semaphore()
    core = dp & 1
    first_core = core == 0
    second_core = core == 1
    chip = dp - core
    gx, gz = dp >> 3, (dp >> 1) & 3
    sy, sz = sp >> 2, sp & 3

    mine = dp >> 1
    mx, mz = mine >> 2, mine & 3
    at_y, at_z = {}, {}
    for ic in range(2):
        c = (core + ic) & 1
        for i in range(4):
            x = (gx + i) & 3
            at_y[i, ic] = (x * 8 + c, x * 2 + c, ((mx - x - 2 * c + 8) & 3) * 4)
            at_z[i, ic] = tri(((1 + 2 * c) * (mz - i + 5)) & 3)
    samples = [
        [
            (at_y[i, ic][0] + 2 * z, at_y[i, ic][1] + 8 * (0, 1, 3, 2)[z], at_y[i, ic][2] + at_z[z, ic])
            for i in (0, 2, 1, 3)
            for ic in range(2)
        ]
        for z in range(4)
    ]

    def hello_holders(z):
        for b, _, s in samples[z][2:]:
            hello(barrier, b | 1, s)
        for b, _, s in samples[z][:2]:

            @pl.when(jnp.logical_or(first_core, jnp.logical_or(gz != z, s != sp)))
            def _():
                hello(barrier, b | 1, s)

    hello_holders(0)
    for k in range(16):

        @pl.when(jnp.logical_or(sp != k, second_core))
        def _():
            hello(barrier, chip, k)

    for z in range(1, 4):
        hello_holders(z)

    own_holder = sp < 0
    for z in range(4):
        for _, _, s in samples[z][:2]:
            own_holder = jnp.logical_or(own_holder, jnp.logical_and(gz == z, s == sp))


    half_way = (sz + 2) & 3
    peer_z = (3 - sz, half_way, 3 - half_way, sz)
    peer_y = tuple((sy + i) & 3 for i in range(4))
    block_y = tuple(((gx + y + 2 * core) & 3) * 4 for y in peer_y)
    block_z = tuple((gz + 3 + (1 + 2 * core) * tri(z)) & 3 for z in peer_z)
    peers = [
        (peer_y[iy] * 4 + peer_z[iz], block_y[iy] + block_z[iz])
        for iz in range(4)
        for iy in (2, 1, 3, 0)
    ]
    my_block = peers[-1][1]
    self_in = my_block == mine
    rank = tri(gz)
    my_slot = rank * 8 + gx * 2 + core
    batch = (3 + 6 * jnp.minimum(rank, 1) + ((rank + 1) >> 2), 4)

    def remote(src, dst, send, recv, b, s):
        pltpu.make_async_remote_copy(
            src_ref=src,
            dst_ref=dst,
            send_sem=send_sem.at[send],
            recv_sem=recv_sem.at[recv],
            device_id=(b, s),
            device_id_type=MESH,
        ).start()

    def local(src, dst, recv):
        pltpu.make_async_copy(src, dst, recv_sem.at[recv]).start()

    def maybe_local(here, src, dst, send, recv, b, s):
        @pl.when(here)
        def _():
            local(src, dst, recv)

        @pl.when(jnp.logical_not(here))
        def _():
            remote(src, dst, send, recv, b, s)

    def arrived(buf, stage):
        with jax.named_scope(f"wait_recv{stage}"):
            pltpu.make_async_copy(buf, buf, recv_sem.at[stage]).wait()

    def yz_modes(k, slab):
        for x in range(4):
            out = dot(yz_v[...], slab[x])
            send1[k, :, x] = out.astype(BF16).reshape(32, 8, C)

    def send_slab(k, c, stage):
        for s, q in peers[:-1]:
            remote(send1.at[k, 16 * c + q], recv1.at[k, 16 * c + sp], stage, stage, dp, s)
        local(send1.at[k, 16 * c + my_block], recv1.at[k, 16 * c + sp], stage)

    def x_modes(k, c):
        slab = recv1[k, pl.ds(16 * c, 16)].reshape(512, C)
        send2[k, pl.ds(16 * c, 16)] = dot(fx_v[...], slab).astype(BF16).reshape(16, 8, C)

    def send_modes(k, c):
        b = 2 * my_block + c
        for i in range(1, 16):
            s = (sp + i) & 15
            remote(send2.at[k, 16 * c + s], recv2.at[k, my_slot], 3 + k, batch[k], b, s)
        here = jnp.logical_and(self_in, core == c)
        maybe_local(
            here, send2.at[k, 16 * c + sp], recv2.at[k, my_slot], 3 + k, batch[k], b, sp
        )

    loads[0].wait()
    loads[1].wait()
    loads += [
        load(2, field_hbm, field_v),
        load(3, fx_hbm, fx_v),
        load(4, w_hbm, w_v),
        load(5, bx_hbm, bx_v),
        load(6, first_hbm, first_v),
        load(7, second_hbm, second_v),
        load(8, zy_hbm, zy_v),
    ]
    yz_modes(0, cot_v)

    with jax.named_scope("wait_barrier"):

        @pl.when(first_core)
        def _():
            pl.semaphore_wait(barrier, 31)
            hello(met.at[0], dp + 1, sp)

        @pl.when(second_core)
        def _():
            pl.semaphore_wait(met.at[0], 1)

    send_slab(0, 0, 0)
    send_slab(0, 1, 1)
    loads[2].wait()
    yz_modes(1, field_v)
    loads[3].wait()
    loads[4].wait()
    half_v[...] = w_v[...].astype(BF16)

    @pl.when(second_core)
    def _():
        @pl.when(own_holder)
        def _():
            pl.semaphore_wait(barrier, 63)

        @pl.when(jnp.logical_not(own_holder))
        def _():
            pl.semaphore_wait(barrier, 64)

        hello(met.at[1], chip, sp)

    def second_chunk():
        arrived(recv1.at[0, pl.ds(16, 16)], 1)
        x_modes(0, 1)

    arrived(recv1.at[0, pl.ds(0, 16)], 0)
    x_modes(0, 0)

    both_first = jnp.logical_and(gz == 0, first_core)

    @pl.when(both_first)
    def _():
        second_chunk()

    @pl.when(first_core)
    def _():
        with jax.named_scope("wait_far0"):
            pl.semaphore_wait(met.at[1], 1)

    send_modes(0, 0)

    @pl.when(jnp.logical_not(both_first))
    def _():
        second_chunk()

    send_modes(0, 1)
    send_slab(1, 0, 2)
    send_slab(1, 1, 2)

    def mode_grads(first, count):
        cot = recv2[0, pl.ds(first, count)].astype(F32).reshape(8 * count, C)
        row = lax.broadcasted_iota(jnp.int32, cot.shape, 0)
        turned = jnp.where(
            lax.rem(row, 2) == 0, pltpu.roll(cot, 8 * count - 1, 0), -pltpu.roll(cot, 1, 0)
        )
        pencil = lax.rem(row // 2, 4)
        back = jnp.zeros(cot.shape, F32)
        for j in range(4):
            for part, rows in ((0, cot), (1, turned)):
                g = jnp.where(pencil == j, rows, 0.0).astype(BF16)
                big_g[pl.ds(8 * first, 8 * count), pl.ds((2 * j + part) * C, C)] = g
                back += lax.dot_general(
                    g, half_v[2 * j + part], (((1,), (1,)), ((), ())), preferred_element_type=F32
                )
        send3[pl.ds(first, count)] = back.astype(BF16).reshape(count, 8, C)

    def send_grads(z):
        for b, slot, s in samples[z][1:]:
            remote(send3.at[slot], recv3.at[core, sp], 5, 5 + core, b, s)
        b, slot, s = samples[z][0]
        here = jnp.logical_and(self_in, gz == z)
        maybe_local(here, send3.at[slot], recv3.at[core, sp], 5, 5 + core, b, s)

    arrived(recv2.at[0, pl.ds(0, 8)], 3)
    mode_grads(0, 8)
    send_grads(0)
    arrived(recv2.at[0, pl.ds(8, 16)], 9)
    mode_grads(8, 16)
    send_grads(1)
    send_grads(3)
    arrived(recv1.at[1], 2)
    for c in range(2):
        x_modes(1, c)
        send_modes(1, c)
    arrived(recv2.at[0, pl.ds(24, 8)], 10)
    mode_grads(24, 8)
    send_grads(2)

    loads[5].wait()
    for c in range(2):
        arrived(recv3.at[c], 5 + c)
        out4 = dot(bx_v[...], recv3[c].reshape(128, C))
        send4[pl.ds(16 * c, 16)] = out4.astype(BF16).reshape(16, 4, 8, C)
        for s, _ in peers[:-1]:
            remote(send4.at[16 * c + s], modes.at[16 * c + my_block], 7 + c, 7 + c, dp, s)
        local(send4.at[16 * c + sp], modes.at[16 * c + my_block], 7 + c)

    loads[6].wait()
    loads[7].wait()
    arrived(recv2.at[1], 4)
    left = recv2[1].astype(F32).reshape(256, C).T.astype(BF16)
    for n in range(8):
        grads = dot(left, big_g[:, pl.ds(n * C, C)])
        new_w[n], new_first[n], new_second[n] = adam_update(
            w_v[n], first_v[n], second_v[n], grads
        )

    def sent(buf, stage):
        pltpu.make_async_copy(buf, buf, send_sem.at[stage]).wait()

    for c in range(2):
        sent(send1.at[0, pl.ds(0, 15)], c)
        sent(send4.at[pl.ds(0, 15)], 7 + c)
    sent(send1.at[1, pl.ds(0, 30)], 2)

    @pl.when(self_in)
    def _():
        for k in range(2):
            sent(send2.at[k, pl.ds(0, 31)], 3 + k)
        sent(send3.at[pl.ds(0, 31)], 5)

    @pl.when(jnp.logical_not(self_in))
    def _():
        for k in range(2):
            sent(send2.at[k], 3 + k)
        sent(send3, 5)

    loads[8].wait()
    for c in range(2):
        arrived(modes.at[pl.ds(16 * c, 16)], 7 + c)
        for x in range(4):
            half = modes[pl.ds(16 * c, 16), x].reshape(128, C)
            term = dot(zy_v[:, pl.ds(128 * c, 128)], half)
            if c == 0:
                part_v[x] = term
            else:
                grad[x] = (part_v[x] + term).astype(BF16)


def exchange(field, cot, weights, first, second, yz, fx, bx, zy):
    any_spec = pl.BlockSpec(memory_space=pl.ANY)
    vmem_spec = pl.BlockSpec(memory_space=pltpu.VMEM)
    part = pltpu.VMEM((8, C, C), F32)
    return pl.pallas_call(
        kernel,
        out_shape=(pltpu.VMEM((4, 512, C), BF16), part, part, part),
        in_specs=[any_spec] * 9,
        out_specs=(vmem_spec,) * 4,
        scratch_shapes=[
            pltpu.VMEM((4, 512, C), BF16),
            pltpu.VMEM((4, 512, C), BF16),
            part,
            part,
            part,
            pltpu.VMEM((256, 512), BF16),
            pltpu.VMEM((128, 512), BF16),
            pltpu.VMEM((512, 128), BF16),
            pltpu.VMEM((512, 256), BF16),
            pltpu.VMEM((8, C, C), BF16),
            pltpu.VMEM((2, 32, 4, 8, C), BF16),
            pltpu.VMEM((2, 32, 4, 8, C), BF16),
            pltpu.VMEM((2, 32, 8, C), BF16),
            pltpu.VMEM((2, 32, 8, C), BF16),
            pltpu.VMEM((256, 1024), BF16),
            pltpu.VMEM((32, 8, C), BF16),
            pltpu.VMEM((2, 16, 8, C), BF16),
            pltpu.VMEM((32, 4, 8, C), BF16),
            pltpu.VMEM((32, 4, 8, C), BF16),
            pltpu.VMEM((4, 512, C), F32),
            pltpu.SemaphoreType.DMA((9,)),
            pltpu.SemaphoreType.DMA((9,)),
            pltpu.SemaphoreType.DMA((11,)),
            pltpu.SemaphoreType.REGULAR((2,)),
        ],
        compiler_params=pltpu.CompilerParams(
            collective_id=0, has_side_effects=True, vmem_limit_bytes=VMEM_GRANT
        ),
    )(field, cot, weights, first, second, yz, fx, bx, zy)


def finish_kernel(*refs):
    sources, targets, sem = refs[:4], refs[4:8], refs[8]
    copies = []
    for src, dst in zip(sources, targets, strict=True):
        rows = src.shape[0] // 4
        for i in range(4):
            span = pl.ds(i * rows, rows)
            copies.append(pltpu.make_async_copy(src.at[span], dst.at[span], sem.at[len(copies)]))
            copies[-1].start()
    for copy in copies:
        copy.wait()


def finish(*results):
    return pl.pallas_call(
        finish_kernel,
        out_shape=tuple(jax.ShapeDtypeStruct(r.shape, r.dtype) for r in results),
        in_specs=[pl.BlockSpec(memory_space=pltpu.VMEM)] * 4,
        out_specs=(pl.BlockSpec(memory_space=pl.ANY),) * 4,
        scratch_shapes=[pltpu.SemaphoreType.DMA((16,))],
        compiler_params=pltpu.CompilerParams(vmem_limit_bytes=16 * 2**20),
    )(*results)


def adam_update(weights, first_moment, second_moment, weight_grads):
    new_first = decay_first * first_moment + (1.0 - decay_first) * weight_grads
    new_second = decay_second * second_moment + (1.0 - decay_second) * weight_grads * weight_grads
    first_hat = new_first / (1.0 - decay_first**STEP)
    second_hat = new_second / (1.0 - decay_second**STEP)
    new_weights = weights - learn_rate * first_hat / (jnp.sqrt(second_hat) + adam_floor)
    return (new_weights, new_first, new_second)


def on_device(field, cotangent, weights, first_moment, second_moment):
    yz, fx, bx, zy = (jnp.asarray(t) for t in tables())
    results = exchange(
        field.reshape(4, 512, C),
        cotangent.reshape(4, 512, C),
        weights.reshape(8, C, C),
        first_moment.reshape(8, C, C),
        second_moment.reshape(8, C, C),
        yz,
        fx,
        bx,
        zy,
    )
    field_grad, *state = finish(*results)
    return (field_grad.reshape(field.shape), *(a.reshape(weights.shape) for a in state))


def solution(mesh):
    placed = (
        P("dp", "space", None, None, None),
        P("dp", "space", None, None, None),
        P("space", "dp", None, None, None),
        P("space", "dp", None, None, None),
        P("space", "dp", None, None, None),
    )
    return jax.shard_map(
        on_device,
        mesh=mesh,
        in_specs=placed,
        out_specs=(
            P("dp", "space", None, None, None),
            P("space", "dp", None, None, None),
            P("space", "dp", None, None, None),
            P("space", "dp", None, None, None),
        ),
        check_vma=False,
    )
```
